32 devices in a mesh: space: 16 (over z, x, core), ens: 2 (over y).
Axes of the slice: x: 2, y: 2, z: 4, core: 2. Of those that a mesh axis runs over, the one named last changes fastest.
Arguments:
- params: float32 [64, 256, 512], P('ens', 'space'), may hold values from 0.55 to 0.8
- base_thickness: float32 [256, 512], P('space'), may hold values from 0.5 to 3
- balance: float32 [256, 512], P('space'), may hold values from -0.1 to 0.3
- step_count: int32 [64], replicated, may hold values from 8 to 32, as said below
- obs_index: int32 [4096], P('space'), may hold values from 0 to 8191
- observed: float32 [4096], P('space'), may hold values from 0.5 to 2
- noise_var: float32 [4096], P('space'), may hold values from 0.5 to 4
Outputs:
- thickness: float32 [64, 256, 512], P('ens', 'space')
- updated: float32 [64, 256, 512], P('ens', 'space')
The draws below stay inside these ranges and needn't reach their ends.
Inputs may be any that keep to these rules, and one draw needn't show every extreme that they name: `step_count`: some member runs exactly 32 steps.
All inputs are finite; a program needn't handle non-finite values.
Results may differ from the reference program's by a relative error of at most 0.000074.
Values sent between devices are 32-bit elements; how exact they have to be, the bound alone decides.
A program may use at most 64 MiB of HBM per device.

```python
import math
import jax
import jax.numpy as jnp
from jax import lax

MEMBERS = 64
CX = 16
NY = 512
OBS_DEV = 256
STEPS = 32
NX = 256
NOBS = 4096


def draw_step_count(key, part):
    first_key, second_key = jax.random.split(jax.random.fold_in(key, 17))
    counts = jax.random.randint(first_key, (MEMBERS,), STEPS // 4, STEPS + 1)
    chosen = jax.random.randint(second_key, (), 0, MEMBERS)
    counts = counts.at[chosen].set(STEPS)
    return counts.astype(jnp.int32)


def draw_params(key, part):
    first_key = jax.random.fold_in(jax.random.fold_in(key, 29), 0)
    shape = (MEMBERS, NX, NY)
    values = jax.random.uniform(first_key, shape, jnp.float32, 0.55, 0.8)
    return values.astype(jnp.float32)


def draw_base_thickness(key, part):
    phase_key, level_key, jitter_key = jax.random.split(jax.random.fold_in(key, 31), 3)
    phase = jax.random.uniform(phase_key, (), jnp.float32, 0.0, 2.0 * math.pi)
    row_pos = jnp.arange(NX, dtype=jnp.float32)[:, None]
    period = 12.0
    high_share = 0.5
    wave = 0.3 * jnp.sin(2.0 * math.pi * row_pos / period + phase)
    upper = jax.random.bernoulli(level_key, high_share, (NX, NY))
    jitter = jax.random.uniform(jitter_key, (NX, NY), jnp.float32, 0.0, 1.0)
    low_value = 0.8 + 0.4 * jitter
    high_value = 2.2 + 0.5 * jitter
    values = jnp.where(upper, high_value, low_value) + wave
    return jnp.clip(values, 0.5, 3.0).astype(jnp.float32)


def touch_ends(array, rng, smallest, largest):
    shape = array.shape
    spot = [jax.random.randint(jax.random.fold_in(rng, axis), (), 0, shape[axis]) for axis in range(len(shape))]
    array = array.at[tuple(spot)].set(smallest)
    longest = shape.index(max(shape))
    spot[longest] = (spot[longest] + 1) % shape[longest]
    return array.at[tuple(spot)].set(largest)


def block_levels(own_key, shape, cuts, low, top_value):
    def one(position, parts):
        draws = jax.random.uniform(jax.random.fold_in(jax.random.fold_in(own_key, 6), position), (parts,), jnp.float32, low / len(cuts), top_value / len(cuts))
        return jnp.repeat(jnp.exp(draws), shape[position] // parts).reshape((-1,) + (1,) * (len(shape) - position - 1))

    factor_of = one(*cuts[0])
    for cut in cuts[1:]:
        factor_of = factor_of * one(*cut)
    return factor_of


def setup_inputs(seed: int = 0) -> dict:
    arg_keys = jax.random.split(jax.random.key(seed), 8)
    params = draw_params(jax.random.fold_in(arg_keys[7], 71), 0)
    base_thickness = draw_base_thickness(jax.random.fold_in(arg_keys[7], 71), 0)
    balance = jnp.clip(-0.1 + 0.4 * jax.random.uniform(arg_keys[2], (NX, NY), jnp.float32) ** block_levels(arg_keys[2], (NX, NY), ((0, 16),), -0.2, 0.2), -0.1, 0.3)
    step_count = draw_step_count(jax.random.fold_in(arg_keys[7], 71), 0)
    obs_index = touch_ends(jax.random.randint(arg_keys[4], (NOBS,), 0, CX * NY), jax.random.fold_in(arg_keys[4], 1), 0, (CX * NY) - 1).astype(jnp.int32)
    observed = jnp.clip(0.5 + 1.5 * jax.random.uniform(arg_keys[5], (NOBS,), jnp.float32) ** block_levels(arg_keys[5], (NOBS,), ((0, 16),), -0.2, 0.2), 0.5, 2.0)
    noise_var = jnp.clip(jnp.exp(math.log(4.0) - 2.0794415 * jax.random.uniform(arg_keys[6], (NOBS,), jnp.float32) ** block_levels(arg_keys[6], (NOBS,), ((0, 16),), -0.2, 0.2)), 0.5, 4.0)
    return {"params": params, "base_thickness": base_thickness, "balance": balance, "step_count": step_count, "obs_index": obs_index, "observed": observed, "noise_var": noise_var}


time_step = 0.11

def stencil(padded, slip_padded, thickness, balance):
    diffusivity = slip_padded * padded * padded / (1.0 + padded * padded)
    centre = diffusivity[:, 1:-1, 1:-1]
    divergence = jnp.zeros_like(thickness)
    for row_part, col_part in ((slice(2, None), slice(1, -1)), (slice(None, -2), slice(1, -1)), (slice(1, -1), slice(2, None)), (slice(1, -1), slice(None, -2))):
        divergence = divergence + 0.5 * (diffusivity[:, row_part, col_part] + centre) * (padded[:, row_part, col_part] - thickness)
    return thickness + time_step * (divergence + balance)

def ensemble_terms(predicted, observed, noise_var):
    members = predicted.shape[0]
    scaling = lax.rsqrt(noise_var)
    average = lax.optimization_barrier(jnp.mean(predicted, axis=0))
    anomalies = (predicted - average) * scaling / jnp.sqrt(jnp.float32(members - 1))
    mismatch = (observed - predicted) * scaling
    gram = jnp.dot(anomalies, anomalies.T, precision=lax.Precision.HIGHEST)
    cross = jnp.dot(anomalies, mismatch.T, precision=lax.Precision.HIGHEST)
    return (gram, cross)

def solve_weights(gram, cross):
    members = gram.shape[0]
    factor = jnp.linalg.cholesky(gram + jnp.eye(members, dtype=gram.dtype))
    inner = lax.linalg.triangular_solve(factor, cross, left_side=True, lower=True)
    result = lax.linalg.triangular_solve(factor, inner, left_side=True, lower=True, transpose_a=True)
    return result / jnp.sqrt(jnp.float32(members - 1))

def reference(params, base_thickness, balance, step_count, obs_index, observed, noise_var):
    members = params.shape[0]
    slip_padded = jnp.pad(jnp.exp(params), ((0, 0), (1, 1), (1, 1)))

    def advance(step_index, thickness):
        padded = jnp.pad(thickness, ((0, 0), (1, 1), (1, 1)))
        moved = stencil(padded, slip_padded, thickness, balance)
        return jnp.where((step_index < step_count)[:, None, None], moved, thickness)
    initial = jnp.broadcast_to(base_thickness[None], params.shape).astype(jnp.float32)
    thickness = lax.fori_loop(0, STEPS, advance, initial)
    block_of = (jnp.arange(NOBS) // OBS_DEV).astype(jnp.int32)
    cell_index = (block_of * (CX * NY) + obs_index).astype(jnp.int32)
    predicted = thickness.reshape(members, NX * NY)[:, cell_index]
    gram, cross = ensemble_terms(predicted, observed, noise_var)
    weights = solve_weights(gram, cross)
    deviation = params - lax.optimization_barrier(jnp.mean(params, axis=0))
    increment = jnp.dot(weights.T, deviation.reshape(members, NX * NY), precision=lax.Precision.HIGHEST)
    updated = params + increment.reshape(params.shape)
    return (thickness, updated)
```

```python
import functools
import jax
import jax.numpy as jnp
from jax import lax
from jax.experimental import pallas as pl
from jax.experimental.pallas import tpu as pltpu
from jax.sharding import PartitionSpec as P

time_step = 0.11
steps = 32
halo = 4
sub = 8
lane = 128
pad = 8
MESH = pl.DeviceIdType.MESH


def reciprocal(x):
    r = pl.reciprocal(x, approx=True)
    return r * (2.0 - x * r)


def dot(left, right, right_dim, left_dim=1):
    return lax.dot_general(
        left, right, (((left_dim,), (right_dim,)), ((), ())),
        precision=lax.Precision.HIGHEST, preferred_element_type=jnp.float32,
    )


def split_pieces(row):
    return [row[:, p * lane : (p + 1) * lane] for p in range(row.shape[1] // lane)]


def swap_piece_and_lane(pieces):
    count = len(pieces)
    lanes = lax.broadcasted_iota(jnp.int32, pieces[0].shape, 1)
    bit = 1
    while bit < count:
        upper = (lanes & bit) > 0
        out = list(pieces)
        for p in range(count):
            if p & bit:
                continue
            low, high = pieces[p], pieces[p + bit]
            out[p] = jnp.where(upper, pltpu.roll(high, bit, 1), low)
            out[p + bit] = jnp.where(upper, high, pltpu.roll(low, lane - bit, 1))
        pieces = out
        bit *= 2
    return pieces


def take_lanes(pieces, index):
    return [jnp.take_along_axis(p, index, axis=1, mode="promise_in_bounds") for p in pieces]


def to_strided(row):
    pieces = swap_piece_and_lane(split_pieces(row))
    count = len(pieces)
    lanes = lax.broadcasted_iota(jnp.int32, pieces[0].shape, 1)
    run = lane // count
    shift = run.bit_length() - 1
    return jnp.concatenate(take_lanes(pieces, (lanes & (run - 1)) * count + (lanes >> shift)), axis=1)


def to_natural(row):
    pieces = split_pieces(row)
    count = len(pieces)
    lanes = lax.broadcasted_iota(jnp.int32, pieces[0].shape, 1)
    shift = count.bit_length() - 1
    index = (lanes & (count - 1)) * (lane // count) + (lanes >> shift)
    return jnp.concatenate(swap_piece_and_lane(take_lanes(pieces, index)), axis=1)


def diffuse(h, slip):
    square = h * h
    return (slip * square) * reciprocal(1.0 + square)


def sweep(source, target, slip_ref, bal_ref, mask, first, count, turns):
    lanes = lax.broadcasted_iota(jnp.int32, (sub, lane), 1)
    at_end = lanes == lane - 1
    at_start = lanes == 0

    def load(row):
        h = source[pad + row]
        return h, diffuse(h, slip_ref[pad + row])

    def body(turn, carry):
        begin = first + turn * count
        h, d, f_up = carry
        for k in range(count):
            row = begin + k
            h_below, d_below = load(row + 1)
            f_down = (d_below + d) * (h_below - h)
            wrapped_h = jnp.where(at_end, 0.0, pltpu.roll(h[:, :lane], lane - 1, 1))
            wrapped_d = jnp.where(at_end, 0.0, pltpu.roll(d[:, :lane], lane - 1, 1))
            h_next = jnp.concatenate([h[:, lane:], wrapped_h], axis=1)
            d_next = jnp.concatenate([d[:, lane:], wrapped_d], axis=1)
            f_right = (d_next + d) * (h_next - h)
            edge = jnp.where(
                at_start, d[:, :lane] * h[:, :lane], pltpu.roll(f_right[:, -lane:], 1, 1)
            )
            f_left = jnp.concatenate([edge, f_right[:, :-lane]], axis=1)
            change = (f_down - f_up) + (f_right - f_left)
            balance = jnp.broadcast_to(bal_ref[pl.ds(pad + row, 1)], h.shape)
            moved = (h + balance) + change
            target[pad + row] = jnp.where(mask(row), moved, h)
            h, d, f_up = h_below, d_below, f_down
        return h, d, f_up

    h_above, d_above = load(first - 1)
    h, d = load(first)
    lax.fori_loop(0, turns, body, (h, d, (d + d_above) * (h - h_above)))


def kernel(
    spaces, enss, params_ref, base_ref, balance_ref, count_ref, index_ref, observed_ref, noise_ref,
    out_ref, updated_ref,
    raw_ref, par_ref, bb_ref, index_land, even_ref, odd_ref, slip_ref, base_c, bal_c, land_ref, sent_ref,
    one_hot_ref, pick_ref, pred_ref, stage_ref, turned_ref, update_ref, sum_ref, sum_land,
    raw_send, raw_recv, bb_send, bb_recv, index_send, index_recv, ens_send, ens_recv, local_sem,
    edge_send, edge_recv, h_send, h_recv, pred_send, pred_recv, thick_send, thick_recv,
    sum_send, sum_recv,
):
    rows, width = base_ref.shape
    members = params_ref.shape[0]
    quad = members // sub
    groups = quad * enss
    total = quad * rows
    every = members * enss
    blocks = steps // halo
    count_obs = index_ref.shape[1]
    pieces = width // lane

    me = lax.axis_index("space")
    ens = lax.axis_index("ens")
    pos = lax.rem(me, quad)
    home = me - pos
    has_up = home > 0
    has_down = home + quad < spaces
    up = jnp.maximum(me - quad, 0)
    down = jnp.minimum(me + quad, spaces - 1)
    sides = ((has_up, up, 1), (has_down, down, 0))

    order = sorted(range(1, quad), key=lambda d: (d % 2, d))
    mates = [lax.rem(pos + d, quad) for d in order]
    others = [lax.rem(ens + d, enss) for d in range(1, enss)]
    peers = [
        (lax.rem(pos + d, quad), lax.rem(ens + e, enss))
        for d in range(quad) for e in range(enss) if d or e
    ]
    stages = spaces.bit_length() - 1
    inner = quad.bit_length() - 1
    bits = [0] + list(range(max(inner, 1), stages)) + list(range(1, inner))
    bits = bits[:stages]
    partners = []
    for stage in bits:
        bit = 1 << stage
        partners.append(me + bit - 2 * bit * lax.rem(lax.div(me, bit), 2))

    barrier = pltpu.get_barrier_semaphore()
    for mate, other in peers:
        pl.semaphore_signal(
            barrier, inc=1, device_id={"space": home + mate, "ens": other}, device_id_type=MESH
        )
    for have, target, _ in sides:
        @pl.when(have)
        def _(target=target):
            pl.semaphore_signal(barrier, inc=1, device_id={"space": target}, device_id_type=MESH)
    outer = [partner for bit, partner in zip(bits, partners) if bit >= inner]
    for partner in outer:
        pl.semaphore_signal(barrier, inc=1, device_id={"space": partner}, device_id_type=MESH)
    own_params = pltpu.make_async_copy(params_ref, par_ref.at[ens], local_sem.at[0])
    own_params.start()
    own_raw = pltpu.make_async_copy(
        params_ref.at[pl.ds(pos * sub, sub)], raw_ref.at[pos], local_sem.at[1]
    )
    own_raw.start()
    pl.semaphore_wait(
        barrier, len(peers) + len(outer) + has_up.astype(jnp.int32) + has_down.astype(jnp.int32)
    )

    def raw_copy(mate, source, slot):
        return pltpu.make_async_remote_copy(
            params_ref.at[pl.ds(mate * sub, sub)], raw_ref.at[source],
            raw_send.at[slot], raw_recv.at[source],
            device_id={"space": home + mate}, device_id_type=MESH,
        )

    def bb_copy(which, mate, source, slot):
        ref = (base_ref, balance_ref)[which]
        return pltpu.make_async_remote_copy(
            ref, bb_ref.at[which, source], bb_send.at[which, slot], bb_recv.at[which, source],
            device_id={"space": home + mate}, device_id_type=MESH,
        )

    def index_copy(mate, source, slot):
        return pltpu.make_async_remote_copy(
            index_ref, index_land.at[source], index_send.at[slot], index_recv.at[source],
            device_id={"space": home + mate}, device_id_type=MESH,
        )

    def ens_copy(step, source):
        return pltpu.make_async_remote_copy(
            params_ref, par_ref.at[source], ens_send.at[step], ens_recv.at[source],
            device_id={"ens": others[step]}, device_id_type=MESH,
        )

    for slot, mate in enumerate(mates):
        for which in range(2):
            bb_copy(which, mate, pos, slot).start()
        raw_copy(mate, pos, slot).start()
    for slot, mate in enumerate(mates):
        index_copy(mate, pos, slot).start()
    for step in range(enss - 1):
        ens_copy(step, ens).start()

    counts = count_ref[...].astype(jnp.float32)
    first_member = ens * members + pos * sub
    mine = (
        lax.broadcasted_iota(jnp.int32, (sub, every), 1)
        == lax.broadcasted_iota(jnp.int32, (sub, every), 0) + first_member
    )
    count = jnp.broadcast_to(
        jnp.sum(jnp.where(mine, jnp.broadcast_to(counts, (sub, every)), 0.0), axis=1, keepdims=True),
        (sub, lane),
    )

    index_land[pos] = index_ref[...]
    bb_ref[0, pos] = base_ref[...]
    bb_ref[1, pos] = balance_ref[...]

    zero = jnp.zeros((sub, width), jnp.float32)
    for side, (have, _, _) in enumerate(sides):
        begin = pad - halo if side == 0 else pad + total

        @pl.when(jnp.logical_not(have))
        def _(side=side, begin=begin):
            for row in range(halo):
                slip_ref[begin + row] = zero
                even_ref[begin + row] = zero
                odd_ref[begin + row] = zero
            edge = 0 if side == 0 else pad + total
            base_c[pl.ds(edge, pad)] = zero
            bal_c[pl.ds(edge, pad)] = zero

    def use_bb(source):
        @pl.loop(0, rows // sub)
        def _(tile):
            at = pl.multiple_of(tile * sub, sub)
            to = pl.multiple_of(pad + source * rows + at, sub)
            base_c[pl.ds(to, sub)] = to_strided(bb_ref[0, source, pl.ds(at, sub)])
            bal_c[pl.ds(to, sub)] = to_strided(bb_ref[1, source, pl.ds(at, sub)] * time_step)

        @pl.loop(0, rows)
        def _(row):
            at = source * rows + row + pad
            even_ref[at] = jnp.broadcast_to(base_c[pl.ds(at, 1)], (sub, width))

    def use_raw(source):
        @pl.loop(0, rows // sub)
        def _(tile):
            at = pl.multiple_of(tile * sub, sub)
            turned = jnp.swapaxes(raw_ref[source, :, pl.ds(at, sub)], 0, 1)
            slip = (jnp.exp(turned) * (0.5 * time_step)).reshape(sub * sub, width)
            slip_ref[pl.ds(pad + source * rows + at, sub)] = to_strided(slip).reshape(sub, sub, width)

    use_bb(pos)
    own_raw.wait()
    use_raw(pos)
    for mate in mates:
        for which in range(2):
            bb_copy(which, mate, mate, 0).wait_recv()
        use_bb(mate)
    for mate in mates:
        index_copy(mate, mate, 0).wait_recv()

    shift = width.bit_length() - 1
    turn = pieces.bit_length() - 1

    def place_of(source):
        index = index_land[source]
        column = index & (width - 1)
        return index >> shift, (column & (pieces - 1)) * lane + (column >> turn)

    @pl.loop(0, quad)
    def _(source):
        _, place = place_of(source)
        one_hot_ref[source] = jnp.where(
            lax.broadcasted_iota(jnp.int32, (width, count_obs), 0) == place, 1.0, 0.0
        ).astype(jnp.bfloat16)

    for mate in reversed(mates):
        raw_copy(mate, mate, 0).wait_recv()
        use_raw(mate)

    def edge_copies(side):
        _, target, there = sides[side]
        slip_from = pad if side == 0 else pad + total - halo
        slip_to = pad + total if side == 0 else pad - halo
        row_from = pad if side == 0 else total
        row_to = pad + total if side == 0 else 0
        pairs = (
            (slip_ref.at[pl.ds(slip_from, halo)], slip_ref.at[pl.ds(slip_to, halo)]),
            (base_c.at[pl.ds(row_from, pad)], base_c.at[pl.ds(row_to, pad)]),
            (bal_c.at[pl.ds(row_from, pad)], bal_c.at[pl.ds(row_to, pad)]),
        )
        return [
            pltpu.make_async_remote_copy(
                source, dest, edge_send.at[side, k], edge_recv.at[there, k],
                device_id={"space": target}, device_id_type=MESH,
            )
            for k, (source, dest) in enumerate(pairs)
        ]

    def edge_arrivals(side):
        _, target, _ = sides[side]
        slip_at = pad - halo if side == 0 else pad + total
        row_at = 0 if side == 0 else pad + total
        refs = (
            slip_ref.at[pl.ds(slip_at, halo)], base_c.at[pl.ds(row_at, pad)],
            bal_c.at[pl.ds(row_at, pad)],
        )
        return [
            pltpu.make_async_remote_copy(
                ref, ref, edge_send.at[side, k], edge_recv.at[side, k],
                device_id={"space": target}, device_id_type=MESH,
            )
            for k, ref in enumerate(refs)
        ]

    for side in range(2):
        @pl.when(sides[side][0])
        def _(side=side):
            for copy in edge_copies(side):
                copy.start()

    def h_copy(side, slot):
        _, target, there = sides[side]
        return pltpu.make_async_remote_copy(
            sent_ref.at[slot, side], land_ref.at[slot, there],
            h_send.at[slot, side], h_recv.at[slot, there],
            device_id={"space": target}, device_id_type=MESH,
        )

    def h_arrival(side, slot):
        _, target, _ = sides[side]
        return pltpu.make_async_remote_copy(
            sent_ref.at[slot, side], land_ref.at[slot, side],
            h_send.at[slot, side], h_recv.at[slot, side],
            device_id={"space": target}, device_id_type=MESH,
        )

    beyond = (count * has_up.astype(jnp.float32), count * has_down.astype(jnp.float32))

    @pl.loop(0, blocks)
    def _(block):
        slot = lax.rem(block, 2)
        begin = (block * halo).astype(jnp.float32)
        buffers = (even_ref, odd_ref)

        def wide(mask):
            return jnp.concatenate([mask] * pieces, axis=1)

        for level in range(1, halo + 1):
            active = wide((begin + float(level - 1)) < count)
            sweep(
                buffers[(level - 1) % 2], buffers[level % 2], slip_ref, bal_c,
                lambda row: active, level, total // 2 - level, 2,
            )

        for side in range(2):
            at = pad - halo if side == 0 else pad + total

            @pl.when(jnp.logical_and(sides[side][0], block == 0))
            def _(side=side, at=at):
                for copy in edge_arrivals(side):
                    copy.wait_recv()
                for row in range(halo):
                    even_ref[at + row] = jnp.broadcast_to(base_c[pl.ds(at + row, 1)], (sub, width))

            @pl.when(jnp.logical_and(sides[side][0], block > 0))
            def _(side=side, at=at):
                h_arrival(side, slot).wait_recv()
                even_ref[pl.ds(at, halo)] = land_ref[slot, side]

            @pl.when(jnp.logical_and(sides[side][0], block > 1))
            def _(side=side):
                h_copy(side, 1 - slot).wait_send()

        @pl.loop(0, halo // 2)
        def _(pair):
            for odd in range(2):
                level = pair * 2 + (odd + 1)
                now = begin + (level - 1).astype(jnp.float32)
                for side in range(2):
                    first = level - halo if side == 0 else total - level

                    def mask(row, side=side, now=now):
                        outside = row < 0 if side == 0 else row >= total
                        return wide(now < jnp.where(outside, beyond[side], count))

                    sweep(
                        buffers[odd], buffers[1 - odd], slip_ref, bal_c, mask, first, halo, 1
                    )

        for side in range(2):
            at = pad if side == 0 else pad + total - halo
            sent_ref[1 - slot, side] = even_ref[pl.ds(at, halo)]

        for side in range(2):
            @pl.when(jnp.logical_and(sides[side][0], block < blocks - 1))
            def _(side=side):
                h_copy(side, 1 - slot).start()

    for source in range(quad):
        cells = even_ref[pl.ds(pad + source * rows, rows)].reshape(rows * sub, width)
        picked = None
        one_hot = one_hot_ref[source]
        for part in range(3):
            cut = cells.astype(jnp.bfloat16)
            if part < 2:
                cells = cells - cut.astype(jnp.float32)
            term = jnp.dot(cut, one_hot, preferred_element_type=jnp.float32)
            picked = term if picked is None else picked + term
        row_at, _ = place_of(source)
        at_row = lax.broadcasted_iota(jnp.int32, (rows, sub, count_obs), 0) == row_at
        pick_ref[source] = jnp.sum(
            jnp.where(at_row, picked.reshape(rows, sub, count_obs), 0.0), axis=0
        )

    def pred_copy(k, source_ens, source_pos):
        mate, other = peers[k]
        return pltpu.make_async_remote_copy(
            pick_ref.at[mate], pred_ref.at[source_ens, source_pos],
            pred_send.at[k], pred_recv.at[source_ens, source_pos],
            device_id={"space": home + mate, "ens": other}, device_id_type=MESH,
        )

    for k in range(len(peers)):
        pred_copy(k, ens, pos).start()
    pred_ref[ens, pos] = pick_ref[pos]

    def thick_copy(mate, source, slot):
        return pltpu.make_async_remote_copy(
            stage_ref.at[mate], out_ref.at[pl.ds(source * sub, sub)],
            thick_send.at[slot], thick_recv.at[source],
            device_id={"space": home + mate}, device_id_type=MESH,
        )

    def unturn(mate):
        @pl.loop(0, rows // sub)
        def _(tile):
            at = pl.multiple_of(tile * sub, sub)
            cells = even_ref[pl.ds(pad + mate * rows + at, sub)].reshape(sub * sub, width)
            stage_ref[mate, :, pl.ds(at, sub)] = jnp.swapaxes(
                to_natural(cells).reshape(sub, sub, width), 0, 1
            )

    for slot, mate in enumerate(mates):
        unturn(mate)
        thick_copy(mate, pos, slot).start()
    unturn(pos)
    own_thick = pltpu.make_async_copy(
        stage_ref.at[pos], out_ref.at[pl.ds(pos * sub, sub)], local_sem.at[2]
    )
    own_thick.start()
    for k, (mate, other) in enumerate(peers):
        pred_copy(k, other, mate).wait_recv()

    scaling = lax.rsqrt(noise_ref[...])
    predicted = pred_ref[...].reshape(every, count_obs)
    average = jnp.sum(predicted, axis=0, keepdims=True) * (1.0 / every)
    root = jnp.sqrt(jnp.float32(every - 1))
    anomalies = (predicted - average) * (scaling / root)
    surprise = (observed_ref[...] - average) * scaling
    spread = sum_ref.shape[2]
    first = lax.broadcasted_iota(jnp.int32, (spread - every, count_obs), 0) == 0
    lower = jnp.where(first, jnp.broadcast_to(surprise, first.shape), 0.0)
    sum_ref[0] = dot(anomalies, jnp.concatenate([anomalies, lower], axis=0), 1)

    def sum_copy(stage):
        return pltpu.make_async_remote_copy(
            sum_ref.at[stage], sum_land.at[stage], sum_send.at[stage], sum_recv.at[stage],
            device_id={"space": partners[stage]}, device_id_type=MESH,
        )

    for stage in range(stages):
        sum_copy(stage).start()
        if stage == 0:
            own_params.wait()
            for step in range(enss - 1):
                ens_copy(step, others[step]).wait_recv()

            @pl.loop(0, groups)
            def _(group):
                member = pl.multiple_of(lax.rem(group, quad) * sub, sub)
                turned_ref[group] = jnp.swapaxes(
                    par_ref[lax.div(group, quad), pl.ds(member, sub)], 0, 1
                )
        sum_copy(stage).wait_recv()
        sum_ref[stage + 1] = sum_ref[stage] + sum_land[stage]

    row_of = lax.broadcasted_iota(jnp.int32, (every, spread), 0)
    lane_of = lax.broadcasted_iota(jnp.int32, (every, spread), 1)
    own_unit = (row_of + (every + 1) == lane_of + ens * members) & (lane_of > every)
    unit = (row_of == lane_of) | own_unit
    system = sum_ref[stages] + jnp.where(unit, 1.0, 0.0)
    for pivot in range(0, every, 2):
        left = jnp.broadcast_to(system[:, pivot : pivot + 1], (every, spread))
        right = jnp.broadcast_to(system[:, pivot + 1 : pivot + 2], (every, spread))
        top, low = system[pivot : pivot + 1], system[pivot + 1 : pivot + 2]
        a, c = left[pivot : pivot + 1], left[pivot + 1 : pivot + 2]
        b, d = right[pivot : pivot + 1], right[pivot + 1 : pivot + 2]
        scale = 1.0 / (a * d - b * c)
        new_top = (d * top - b * low) * scale
        new_low = (a * low - c * top) * scale
        rest = system - left * new_top - right * new_low
        system = jnp.where(
            row_of == pivot, new_top, jnp.where(row_of == pivot + 1, new_low, rest)
        )
    gain = system[:, every : every + 1] / root
    weights = system[:, every + 1 : every + 1 + members] + gain
    weights = weights - jnp.where(
        lax.broadcasted_iota(jnp.int32, (every, members), 0)
        == lax.broadcasted_iota(jnp.int32, (every, members), 1) + ens * members, 1.0, 0.0,
    )
    weights = weights - jnp.sum(weights, axis=0, keepdims=True) * (1.0 / every)
    weights = weights.T

    @pl.loop(0, rows)
    def _(row):
        block = turned_ref[:, row].reshape(every, width)
        own = turned_ref[pl.ds(ens * quad, quad), row]
        update_ref[:, row] = own + dot(weights, block, 0).reshape(quad, sub, width)

    for group in range(quad):
        updated_ref[pl.ds(group * sub, sub)] = jnp.swapaxes(update_ref[group], 0, 1)

    for mate in mates:
        thick_copy(mate, mate, 0).wait_recv()
    own_thick.wait()
    for slot, mate in enumerate(mates):
        for which in range(2):
            bb_copy(which, mate, pos, slot).wait_send()
        raw_copy(mate, pos, slot).wait_send()
        index_copy(mate, pos, slot).wait_send()
        thick_copy(mate, pos, slot).wait_send()
    for step in range(enss - 1):
        ens_copy(step, ens).wait_send()
    for k in range(len(peers)):
        pred_copy(k, ens, pos).wait_send()
    for stage in range(stages):
        sum_copy(stage).wait_send()
    for side in range(2):
        @pl.when(sides[side][0])
        def _(side=side):
            for copy in edge_copies(side):
                copy.wait_send()
            h_copy(side, (blocks - 1) % 2).wait_send()


def shards(params, base_thickness, balance, step_count, obs_index, observed, noise_var):
    members, rows, width = params.shape
    spaces, enss = lax.axis_size("space"), lax.axis_size("ens")
    quad = members // sub
    total = quad * rows
    every = members * enss
    count_obs = obs_index.shape[0]
    spread = pl.cdiv(every + 1 + members, lane) * lane
    stages = spaces.bit_length() - 1
    assert 1 << stages == spaces and spaces % quad == 0 and quad & (quad - 1) == 0
    assert width & (width - 1) == 0 and steps // halo > 2
    dma = pltpu.SemaphoreType.DMA
    vmem = pl.BlockSpec(memory_space=pltpu.VMEM)
    f32 = jnp.float32
    many = max(quad - 1, 1)
    flat = jax.ShapeDtypeStruct(params.shape, f32)
    return pl.pallas_call(
        functools.partial(kernel, spaces, enss),
        out_shape=(flat, flat),
        in_specs=[pl.BlockSpec(memory_space=pl.ANY)] + [vmem] * 6,
        out_specs=(vmem, vmem),
        scratch_shapes=[
            pltpu.VMEM((quad, sub, rows, width), f32),
            pltpu.VMEM((enss, members, rows, width), f32),
            pltpu.VMEM((2, quad, rows, width), f32),
            pltpu.VMEM((quad, 1, count_obs), jnp.int32),
            pltpu.VMEM((total + 2 * pad, sub, width), f32),
            pltpu.VMEM((total + 2 * pad, sub, width), f32),
            pltpu.VMEM((total + 2 * pad, sub, width), f32),
            pltpu.VMEM((total + 2 * pad, width), f32),
            pltpu.VMEM((total + 2 * pad, width), f32),
            pltpu.VMEM((2, 2, halo, sub, width), f32),
            pltpu.VMEM((2, 2, halo, sub, width), f32),
            pltpu.VMEM((quad, width, count_obs), jnp.bfloat16),
            pltpu.VMEM((quad, sub, count_obs), f32),
            pltpu.VMEM((enss, quad, sub, count_obs), f32),
            pltpu.VMEM((quad, sub, rows, width), f32),
            pltpu.VMEM((quad * enss, rows, sub, width), f32),
            pltpu.VMEM((quad, rows, sub, width), f32),
            pltpu.VMEM((stages + 1, every, spread), f32),
            pltpu.VMEM((stages, every, spread), f32),
            dma((many,)), dma((quad,)),
            dma((2, many)), dma((2, quad)),
            dma((many,)), dma((quad,)),
            dma((max(enss - 1, 1),)), dma((enss,)),
            dma((3,)),
            dma((2, 3)), dma((2, 3)),
            dma((2, 2)), dma((2, 2)),
            dma((quad * enss,)), dma((enss, quad)),
            dma((many,)), dma((quad,)),
            dma((stages,)), dma((stages,)),
        ],
        compiler_params=pltpu.CompilerParams(
            collective_id=0, has_side_effects=True, vmem_limit_bytes=48 * 1024 * 1024
        ),
        name="advance",
    )(
        params, base_thickness, balance, step_count[None],
        obs_index[None], observed[None], noise_var[None],
    )


def solution(mesh):
    in_specs = (
        P("ens", "space", None),
        P("space", None),
        P("space", None),
        P(),
        P("space"),
        P("space"),
        P("space"),
    )
    out_specs = (P("ens", "space", None), P("ens", "space", None))
    return jax.shard_map(shards, mesh=mesh, in_specs=in_specs, out_specs=out_specs, check_vma=False)
```

```python
import functools
import jax
import jax.numpy as jnp
from jax import lax
from jax.experimental import pallas as pl
from jax.experimental.pallas import tpu as pltpu
from jax.sharding import PartitionSpec as P

time_step = 0.11
steps = 32
halo = 8
sub = 8
lane = 128
pad = 8
MESH = pl.DeviceIdType.MESH


def dot(left, right, right_dim, left_dim=1):
    return lax.dot_general(
        left, right, (((left_dim,), (right_dim,)), ((), ())),
        precision=lax.Precision.HIGHEST, preferred_element_type=jnp.float32,
    )


def split_pieces(row):
    return [row[:, p * lane : (p + 1) * lane] for p in range(row.shape[1] // lane)]


def swap_piece_and_lane(pieces):
    count = len(pieces)
    lanes = lax.broadcasted_iota(jnp.int32, pieces[0].shape, 1)
    bit = 1
    while bit < count:
        upper = (lanes & bit) > 0
        out = list(pieces)
        for p in range(count):
            if p & bit:
                continue
            low, high = pieces[p], pieces[p + bit]
            out[p] = jnp.where(upper, pltpu.roll(high, bit, 1), low)
            out[p + bit] = jnp.where(upper, high, pltpu.roll(low, lane - bit, 1))
        pieces = out
        bit *= 2
    return pieces


def take_lanes(pieces, index):
    return [jnp.take_along_axis(p, index, axis=1, mode="promise_in_bounds") for p in pieces]


def to_strided(row):
    pieces = swap_piece_and_lane(split_pieces(row))
    count = len(pieces)
    lanes = lax.broadcasted_iota(jnp.int32, pieces[0].shape, 1)
    run = lane // count
    shift = run.bit_length() - 1
    return jnp.concatenate(take_lanes(pieces, (lanes & (run - 1)) * count + (lanes >> shift)), axis=1)


def to_natural(row):
    pieces = split_pieces(row)
    count = len(pieces)
    lanes = lax.broadcasted_iota(jnp.int32, pieces[0].shape, 1)
    shift = count.bit_length() - 1
    index = (lanes & (count - 1)) * (lane // count) + (lanes >> shift)
    return jnp.concatenate(swap_piece_and_lane(take_lanes(pieces, index)), axis=1)


def diffuse(h, slip):
    square = h * h
    return (slip * square) * pl.reciprocal(1.0 + square, approx=True)


def sweep(source, target, slip_ref, bal_ref, mask, first, count, turns):
    lanes = lax.broadcasted_iota(jnp.int32, (sub, lane), 1)
    at_end = lanes == lane - 1
    at_start = lanes == 0

    def load(row):
        h = source[pad + row]
        return h, diffuse(h, slip_ref[pad + row])

    def body(turn, carry):
        begin = first + turn * count
        h, d, f_up = carry
        for k in range(count):
            row = begin + k
            h_below, d_below = load(row + 1)
            f_down = (d_below + d) * (h_below - h)
            wrapped_h = jnp.where(at_end, 0.0, pltpu.roll(h[:, :lane], lane - 1, 1))
            wrapped_d = jnp.where(at_end, 0.0, pltpu.roll(d[:, :lane], lane - 1, 1))
            h_next = jnp.concatenate([h[:, lane:], wrapped_h], axis=1)
            d_next = jnp.concatenate([d[:, lane:], wrapped_d], axis=1)
            f_right = (d_next + d) * (h_next - h)
            edge = jnp.where(
                at_start, d[:, :lane] * h[:, :lane], pltpu.roll(f_right[:, -lane:], 1, 1)
            )
            f_left = jnp.concatenate([edge, f_right[:, :-lane]], axis=1)
            change = (f_down - f_up) + (f_right - f_left)
            balance = jnp.broadcast_to(bal_ref[pl.ds(pad + row, 1)], h.shape)
            moved = (h + balance) + change
            target[pad + row] = jnp.where(mask(row), moved, h)
            h, d, f_up = h_below, d_below, f_down
        return h, d, f_up

    h_above, d_above = load(first - 1)
    h, d = load(first)
    carry = (h, d, (d + d_above) * (h - h_above))
    if turns == 1:
        body(0, carry)
    else:
        lax.fori_loop(0, turns, body, carry)


def kernel(
    spaces, enss, params_ref, base_hbm, balance_hbm, count_hbm, index_hbm, observed_hbm, noise_hbm,
    out_ref, updated_ref,
    count_ref, observed_ref, noise_ref, raw_ref, par_ref, bb_ref, index_land, even_ref, odd_ref, slip_ref, base_c, bal_c, land_ref, sent_ref,
    one_hot_ref, pick_ref, pred_ref, stage_ref, turned_ref, update_ref, sum_ref, sum_land,
    raw_send, raw_recv, bb_send, bb_recv, index_send, index_recv, ens_send, ens_recv, local_sem,
    edge_send, edge_recv, h_send, h_recv, pred_send, pred_recv, thick_send, thick_recv,
    sum_send, sum_recv,
):
    rows, width = base_hbm.shape
    members = params_ref.shape[0]
    quad = members // sub
    groups = quad * enss
    total = quad * rows
    every = members * enss
    blocks = steps // halo
    count_obs = index_hbm.shape[1]
    pieces = width // lane

    me = lax.axis_index("space")
    ens = lax.axis_index("ens")
    pos = lax.rem(me, quad)
    home = me - pos
    has_up = home > 0
    has_down = home + quad < spaces
    up = jnp.maximum(me - quad, 0)
    down = jnp.minimum(me + quad, spaces - 1)
    sides = ((has_up, up, 1), (has_down, down, 0))

    order = sorted(range(1, quad), key=lambda d: (d % 2, d))
    mates = [lax.rem(pos + d, quad) for d in order]
    others = [lax.rem(ens + d, enss) for d in range(1, enss)]
    peers = [
        (lax.rem(pos + d, quad), lax.rem(ens + e, enss))
        for d in range(quad) for e in range(enss) if d or e
    ]
    stages = spaces.bit_length() - 1
    inner = quad.bit_length() - 1
    bits = [0] + list(range(max(inner, 1), stages)) + list(range(1, inner))
    bits = bits[:stages]
    partners = []
    for stage in bits:
        bit = 1 << stage
        partners.append(me + bit - 2 * bit * lax.rem(lax.div(me, bit), 2))

    fetches = [
        pltpu.make_async_copy(source, dest, local_sem.at[k])
        for k, (source, dest) in enumerate((
            (params_ref.at[pl.ds(pos * sub, sub)], raw_ref.at[pos]),
            (base_hbm, bb_ref.at[0, pos]),
            (balance_hbm, bb_ref.at[1, pos]),
            (count_hbm, count_ref),
            (index_hbm, index_land.at[pos]),
            (observed_hbm, observed_ref),
            (noise_hbm, noise_ref),
            (params_ref, par_ref.at[ens]),
        ))
    ]
    own_raw, own_params = fetches[0], fetches[-1]
    barrier = pltpu.get_barrier_semaphore()
    for mate, other in peers:
        pl.semaphore_signal(
            barrier, inc=1, device_id={"space": home + mate, "ens": other}, device_id_type=MESH
        )
    for have, target, _ in sides:
        @pl.when(have)
        def _(target=target):
            pl.semaphore_signal(barrier, inc=1, device_id={"space": target}, device_id_type=MESH)
    outer = [partner for bit, partner in zip(bits, partners) if bit >= inner]
    for partner in outer:
        pl.semaphore_signal(barrier, inc=1, device_id={"space": partner}, device_id_type=MESH)
    for fetch in fetches:
        fetch.start()
    pl.semaphore_wait(
        barrier, len(peers) + len(outer) + has_up.astype(jnp.int32) + has_down.astype(jnp.int32)
    )

    def raw_copy(mate, source, slot):
        return pltpu.make_async_remote_copy(
            params_ref.at[pl.ds(mate * sub, sub)], raw_ref.at[source],
            raw_send.at[slot], raw_recv.at[source],
            device_id={"space": home + mate}, device_id_type=MESH,
        )

    def bb_copy(which, mate, source, slot):
        ref = (base_hbm, balance_hbm)[which]
        return pltpu.make_async_remote_copy(
            ref, bb_ref.at[which, source], bb_send.at[which, slot], bb_recv.at[which, source],
            device_id={"space": home + mate}, device_id_type=MESH,
        )

    def index_copy(mate, source, slot):
        return pltpu.make_async_remote_copy(
            index_hbm, index_land.at[source], index_send.at[slot], index_recv.at[source],
            device_id={"space": home + mate}, device_id_type=MESH,
        )

    def ens_copy(step, source):
        return pltpu.make_async_remote_copy(
            params_ref, par_ref.at[source], ens_send.at[step], ens_recv.at[source],
            device_id={"ens": others[step]}, device_id_type=MESH,
        )

    for slot, mate in enumerate(mates):
        for which in range(2):
            bb_copy(which, mate, pos, slot).start()
        raw_copy(mate, pos, slot).start()
    for slot, mate in enumerate(mates):
        index_copy(mate, pos, slot).start()
    for step in range(enss - 1):
        ens_copy(step, ens).start()

    for fetch in fetches[1:-1]:
        fetch.wait()
    counts = count_ref[...].astype(jnp.float32)
    first_member = ens * members + pos * sub
    mine = (
        lax.broadcasted_iota(jnp.int32, (sub, every), 1)
        == lax.broadcasted_iota(jnp.int32, (sub, every), 0) + first_member
    )
    count = jnp.broadcast_to(
        jnp.sum(jnp.where(mine, jnp.broadcast_to(counts, (sub, every)), 0.0), axis=1, keepdims=True),
        (sub, lane),
    )

    zero = jnp.zeros((sub, width), jnp.float32)
    for side, (have, _, _) in enumerate(sides):
        begin = pad - halo if side == 0 else pad + total

        @pl.when(jnp.logical_not(have))
        def _(side=side, begin=begin):
            for row in range(halo):
                slip_ref[begin + row] = zero
                even_ref[begin + row] = zero
                odd_ref[begin + row] = zero
            edge = 0 if side == 0 else pad + total
            base_c[pl.ds(edge, pad)] = zero
            bal_c[pl.ds(edge, pad)] = zero

    def use_bb(source):
        @pl.loop(0, rows // sub)
        def _(tile):
            at = pl.multiple_of(tile * sub, sub)
            to = pl.multiple_of(pad + source * rows + at, sub)
            base_c[pl.ds(to, sub)] = to_strided(bb_ref[0, source, pl.ds(at, sub)])
            bal_c[pl.ds(to, sub)] = to_strided(bb_ref[1, source, pl.ds(at, sub)] * time_step)

        @pl.loop(0, rows)
        def _(row):
            at = source * rows + row + pad
            even_ref[at] = jnp.broadcast_to(base_c[pl.ds(at, 1)], (sub, width))

    def use_raw(source):
        @pl.loop(0, rows // sub)
        def _(tile):
            at = pl.multiple_of(tile * sub, sub)
            turned = jnp.swapaxes(raw_ref[source, :, pl.ds(at, sub)], 0, 1)
            slip = (jnp.exp(turned) * (0.5 * time_step)).reshape(sub * sub, width)
            slip_ref[pl.ds(pad + source * rows + at, sub)] = to_strided(slip).reshape(sub, sub, width)

    use_bb(pos)
    own_raw.wait()
    use_raw(pos)
    for mate in mates:
        for which in range(2):
            bb_copy(which, mate, mate, 0).wait_recv()
        use_bb(mate)
    for mate in mates:
        index_copy(mate, mate, 0).wait_recv()

    shift = width.bit_length() - 1
    turn = pieces.bit_length() - 1

    def place_of(source):
        index = index_land[source]
        column = index & (width - 1)
        return index >> shift, (column & (pieces - 1)) * lane + (column >> turn)

    @pl.loop(0, quad)
    def _(source):
        _, place = place_of(source)
        one_hot_ref[source] = jnp.where(
            lax.broadcasted_iota(jnp.int32, (width, count_obs), 0) == place, 1.0, 0.0
        ).astype(jnp.bfloat16)

    for mate in reversed(mates):
        raw_copy(mate, mate, 0).wait_recv()
        use_raw(mate)

    def edge_copies(side):
        _, target, there = sides[side]
        slip_from = pad if side == 0 else pad + total - halo
        slip_to = pad + total if side == 0 else pad - halo
        row_from = pad if side == 0 else total
        row_to = pad + total if side == 0 else 0
        pairs = (
            (slip_ref.at[pl.ds(slip_from, halo)], slip_ref.at[pl.ds(slip_to, halo)]),
            (base_c.at[pl.ds(row_from, pad)], base_c.at[pl.ds(row_to, pad)]),
            (bal_c.at[pl.ds(row_from, pad)], bal_c.at[pl.ds(row_to, pad)]),
        )
        return [
            pltpu.make_async_remote_copy(
                source, dest, edge_send.at[side, k], edge_recv.at[there, k],
                device_id={"space": target}, device_id_type=MESH,
            )
            for k, (source, dest) in enumerate(pairs)
        ]

    def edge_arrivals(side):
        _, target, _ = sides[side]
        slip_at = pad - halo if side == 0 else pad + total
        row_at = 0 if side == 0 else pad + total
        refs = (
            slip_ref.at[pl.ds(slip_at, halo)], base_c.at[pl.ds(row_at, pad)],
            bal_c.at[pl.ds(row_at, pad)],
        )
        return [
            pltpu.make_async_remote_copy(
                ref, ref, edge_send.at[side, k], edge_recv.at[side, k],
                device_id={"space": target}, device_id_type=MESH,
            )
            for k, ref in enumerate(refs)
        ]

    for side in range(2):
        @pl.when(sides[side][0])
        def _(side=side):
            for copy in edge_copies(side):
                copy.start()

    def h_copy(side, slot):
        _, target, there = sides[side]
        return pltpu.make_async_remote_copy(
            sent_ref.at[slot, side], land_ref.at[slot, there],
            h_send.at[slot, side], h_recv.at[slot, there],
            device_id={"space": target}, device_id_type=MESH,
        )

    def h_arrival(side, slot):
        _, target, _ = sides[side]
        return pltpu.make_async_remote_copy(
            sent_ref.at[slot, side], land_ref.at[slot, side],
            h_send.at[slot, side], h_recv.at[slot, side],
            device_id={"space": target}, device_id_type=MESH,
        )

    beyond = (count * has_up.astype(jnp.float32), count * has_down.astype(jnp.float32))

    @pl.loop(0, blocks)
    def _(block):
        slot = lax.rem(block, 2)
        begin = (block * halo).astype(jnp.float32)
        buffers = (even_ref, odd_ref)

        def wide(mask):
            return jnp.concatenate([mask] * pieces, axis=1)

        for level in range(1, halo + 1):
            active = wide((begin + float(level - 1)) < count)
            sweep(
                buffers[(level - 1) % 2], buffers[level % 2], slip_ref, bal_c,
                lambda row: active, level, total // 2 - level, 2,
            )

        for side in range(2):
            at = pad - halo if side == 0 else pad + total

            @pl.when(jnp.logical_and(sides[side][0], block == 0))
            def _(side=side, at=at):
                for copy in edge_arrivals(side):
                    copy.wait_recv()
                for row in range(halo):
                    even_ref[at + row] = jnp.broadcast_to(base_c[pl.ds(at + row, 1)], (sub, width))

            @pl.when(jnp.logical_and(sides[side][0], block > 0))
            def _(side=side, at=at):
                h_arrival(side, slot).wait_recv()
                even_ref[pl.ds(at, halo)] = land_ref[slot, side]

            @pl.when(jnp.logical_and(sides[side][0], block > 1))
            def _(side=side):
                h_copy(side, 1 - slot).wait_send()

        @pl.loop(0, halo // 2)
        def _(pair):
            for odd in range(2):
                level = pair * 2 + (odd + 1)
                now = begin + (level - 1).astype(jnp.float32)
                for side in range(2):
                    first = level - halo if side == 0 else total - level

                    def mask(row, side=side, now=now):
                        outside = row < 0 if side == 0 else row >= total
                        return wide(now < jnp.where(outside, beyond[side], count))

                    sweep(
                        buffers[odd], buffers[1 - odd], slip_ref, bal_c, mask, first, halo, 1
                    )

        for side in range(2):
            at = pad if side == 0 else pad + total - halo
            sent_ref[1 - slot, side] = even_ref[pl.ds(at, halo)]

        for side in range(2):
            @pl.when(jnp.logical_and(sides[side][0], block < blocks - 1))
            def _(side=side):
                h_copy(side, 1 - slot).start()

    for source in range(quad):
        cells = even_ref[pl.ds(pad + source * rows, rows)].reshape(rows * sub, width)
        picked = None
        one_hot = one_hot_ref[source]
        for part in range(3):
            cut = cells.astype(jnp.bfloat16)
            if part < 2:
                cells = cells - cut.astype(jnp.float32)
            term = jnp.dot(cut, one_hot, preferred_element_type=jnp.float32)
            picked = term if picked is None else picked + term
        row_at, _ = place_of(source)
        at_row = lax.broadcasted_iota(jnp.int32, (rows, sub, count_obs), 0) == row_at
        pick_ref[source] = jnp.sum(
            jnp.where(at_row, picked.reshape(rows, sub, count_obs), 0.0), axis=0
        )

    def pred_copy(k, source_ens, source_pos):
        mate, other = peers[k]
        return pltpu.make_async_remote_copy(
            pick_ref.at[mate], pred_ref.at[source_ens, source_pos],
            pred_send.at[k], pred_recv.at[source_ens, source_pos],
            device_id={"space": home + mate, "ens": other}, device_id_type=MESH,
        )

    for k in range(len(peers)):
        pred_copy(k, ens, pos).start()
    pred_ref[ens, pos] = pick_ref[pos]

    def thick_copy(mate, source, slot):
        return pltpu.make_async_remote_copy(
            stage_ref.at[mate], out_ref.at[pl.ds(source * sub, sub)],
            thick_send.at[slot], thick_recv.at[source],
            device_id={"space": home + mate}, device_id_type=MESH,
        )

    def unturn(mate):
        @pl.loop(0, rows // sub)
        def _(tile):
            at = pl.multiple_of(tile * sub, sub)
            cells = even_ref[pl.ds(pad + mate * rows + at, sub)].reshape(sub * sub, width)
            stage_ref[mate, :, pl.ds(at, sub)] = jnp.swapaxes(
                to_natural(cells).reshape(sub, sub, width), 0, 1
            )

    for slot, mate in enumerate(mates):
        unturn(mate)
        thick_copy(mate, pos, slot).start()
    unturn(pos)
    own_thick = pltpu.make_async_copy(
        stage_ref.at[pos], out_ref.at[pl.ds(pos * sub, sub)], local_sem.at[8]
    )
    own_thick.start()
    for k, (mate, other) in enumerate(peers):
        pred_copy(k, other, mate).wait_recv()

    scaling = lax.rsqrt(noise_ref[...])
    predicted = pred_ref[...].reshape(every, count_obs)
    average = jnp.sum(predicted, axis=0, keepdims=True) * (1.0 / every)
    root = jnp.sqrt(jnp.float32(every - 1))
    anomalies = (predicted - average) * (scaling / root)
    surprise = (observed_ref[...] - average) * scaling
    spread = sum_ref.shape[2]
    first = lax.broadcasted_iota(jnp.int32, (spread - every, count_obs), 0) == 0
    lower = jnp.where(first, jnp.broadcast_to(surprise, first.shape), 0.0)
    sum_ref[0] = dot(anomalies, jnp.concatenate([anomalies, lower], axis=0), 1)

    def sum_copy(stage):
        return pltpu.make_async_remote_copy(
            sum_ref.at[stage], sum_land.at[stage], sum_send.at[stage], sum_recv.at[stage],
            device_id={"space": partners[stage]}, device_id_type=MESH,
        )

    for stage in range(stages):
        sum_copy(stage).start()
        if stage == 0:
            own_params.wait()
            for step in range(enss - 1):
                ens_copy(step, others[step]).wait_recv()

            @pl.loop(0, groups)
            def _(group):
                member = pl.multiple_of(lax.rem(group, quad) * sub, sub)
                turned_ref[group] = jnp.swapaxes(
                    par_ref[lax.div(group, quad), pl.ds(member, sub)], 0, 1
                )
        sum_copy(stage).wait_recv()
        sum_ref[stage + 1] = sum_ref[stage] + sum_land[stage]

    row_of = lax.broadcasted_iota(jnp.int32, (every, spread), 0)
    lane_of = lax.broadcasted_iota(jnp.int32, (every, spread), 1)
    own_unit = (row_of + (every + 1) == lane_of + ens * members) & (lane_of > every)
    unit = (row_of == lane_of) | own_unit
    system = sum_ref[stages] + jnp.where(unit, 1.0, 0.0)
    for pivot in range(0, every, 2):
        left = jnp.broadcast_to(system[:, pivot : pivot + 1], (every, spread))
        right = jnp.broadcast_to(system[:, pivot + 1 : pivot + 2], (every, spread))
        top, low = system[pivot : pivot + 1], system[pivot + 1 : pivot + 2]
        a, c = left[pivot : pivot + 1], left[pivot + 1 : pivot + 2]
        b, d = right[pivot : pivot + 1], right[pivot + 1 : pivot + 2]
        scale = 1.0 / (a * d - b * c)
        new_top = (d * top - b * low) * scale
        new_low = (a * low - c * top) * scale
        rest = system - left * new_top - right * new_low
        system = jnp.where(
            row_of == pivot, new_top, jnp.where(row_of == pivot + 1, new_low, rest)
        )
    gain = system[:, every : every + 1] / root
    weights = system[:, every + 1 : every + 1 + members] + gain
    weights = weights - jnp.where(
        lax.broadcasted_iota(jnp.int32, (every, members), 0)
        == lax.broadcasted_iota(jnp.int32, (every, members), 1) + ens * members, 1.0, 0.0,
    )
    weights = weights - jnp.sum(weights, axis=0, keepdims=True) * (1.0 / every)
    weights = weights.T

    @pl.loop(0, rows)
    def _(row):
        block = turned_ref[:, row].reshape(every, width)
        own = turned_ref[pl.ds(ens * quad, quad), row]
        update_ref[:, row] = own + dot(weights, block, 0).reshape(quad, sub, width)

    for group in range(quad):
        updated_ref[pl.ds(group * sub, sub)] = jnp.swapaxes(update_ref[group], 0, 1)

    for mate in mates:
        thick_copy(mate, mate, 0).wait_recv()
    own_thick.wait()
    for slot, mate in enumerate(mates):
        for which in range(2):
            bb_copy(which, mate, pos, slot).wait_send()
        raw_copy(mate, pos, slot).wait_send()
        index_copy(mate, pos, slot).wait_send()
        thick_copy(mate, pos, slot).wait_send()
    for step in range(enss - 1):
        ens_copy(step, ens).wait_send()
    for k in range(len(peers)):
        pred_copy(k, ens, pos).wait_send()
    for stage in range(stages):
        sum_copy(stage).wait_send()
    for side in range(2):
        @pl.when(sides[side][0])
        def _(side=side):
            for copy in edge_copies(side):
                copy.wait_send()
            h_copy(side, (blocks - 1) % 2).wait_send()


def shards(params, base_thickness, balance, step_count, obs_index, observed, noise_var):
    members, rows, width = params.shape
    spaces, enss = lax.axis_size("space"), lax.axis_size("ens")
    quad = members // sub
    total = quad * rows
    every = members * enss
    count_obs = obs_index.shape[0]
    spread = pl.cdiv(every + 1 + members, lane) * lane
    stages = spaces.bit_length() - 1
    assert 1 << stages == spaces and spaces % quad == 0 and quad & (quad - 1) == 0
    assert width & (width - 1) == 0 and steps // halo > 2
    dma = pltpu.SemaphoreType.DMA
    vmem = pl.BlockSpec(memory_space=pltpu.VMEM)
    f32 = jnp.float32
    many = max(quad - 1, 1)
    flat = jax.ShapeDtypeStruct(params.shape, f32)
    return pl.pallas_call(
        functools.partial(kernel, spaces, enss),
        out_shape=(flat, flat),
        in_specs=[pl.BlockSpec(memory_space=pltpu.HBM)] * 7,
        out_specs=(vmem, vmem),
        scratch_shapes=[
            pltpu.VMEM((1, every), jnp.int32),
            pltpu.VMEM((1, count_obs), f32),
            pltpu.VMEM((1, count_obs), f32),
            pltpu.VMEM((quad, sub, rows, width), f32),
            pltpu.VMEM((enss, members, rows, width), f32),
            pltpu.VMEM((2, quad, rows, width), f32),
            pltpu.VMEM((quad, 1, count_obs), jnp.int32),
            pltpu.VMEM((total + 2 * pad, sub, width), f32),
            pltpu.VMEM((total + 2 * pad, sub, width), f32),
            pltpu.VMEM((total + 2 * pad, sub, width), f32),
            pltpu.VMEM((total + 2 * pad, width), f32),
            pltpu.VMEM((total + 2 * pad, width), f32),
            pltpu.VMEM((2, 2, halo, sub, width), f32),
            pltpu.VMEM((2, 2, halo, sub, width), f32),
            pltpu.VMEM((quad, width, count_obs), jnp.bfloat16),
            pltpu.VMEM((quad, sub, count_obs), f32),
            pltpu.VMEM((enss, quad, sub, count_obs), f32),
            pltpu.VMEM((quad, sub, rows, width), f32),
            pltpu.VMEM((quad * enss, rows, sub, width), f32),
            pltpu.VMEM((quad, rows, sub, width), f32),
            pltpu.VMEM((stages + 1, every, spread), f32),
            pltpu.VMEM((stages, every, spread), f32),
            dma((many,)), dma((quad,)),
            dma((2, many)), dma((2, quad)),
            dma((many,)), dma((quad,)),
            dma((max(enss - 1, 1),)), dma((enss,)),
            dma((9,)),
            dma((2, 3)), dma((2, 3)),
            dma((2, 2)), dma((2, 2)),
            dma((quad * enss,)), dma((enss, quad)),
            dma((many,)), dma((quad,)),
            dma((stages,)), dma((stages,)),
        ],
        compiler_params=pltpu.CompilerParams(
            collective_id=0, has_side_effects=True, vmem_limit_bytes=48 * 1024 * 1024
        ),
        name="advance",
    )(
        *(pltpu.with_memory_space_constraint(x, pltpu.HBM) for x in (
            params, base_thickness, balance, step_count[None],
            obs_index[None], observed[None], noise_var[None],
        ))
    )


def solution(mesh):
    in_specs = (
        P("ens", "space", None),
        P("space", None),
        P("space", None),
        P(),
        P("space"),
        P("space"),
        P("space"),
    )
    out_specs = (P("ens", "space", None), P("ens", "space", None))
    return jax.shard_map(shards, mesh=mesh, in_specs=in_specs, out_specs=out_specs, check_vma=False)
```

```python
import functools
import jax
import jax.numpy as jnp
from jax import lax
from jax.experimental import pallas as pl
from jax.experimental.pallas import tpu as pltpu
from jax.sharding import PartitionSpec as P

time_step = 0.11
steps = 32
halo = 8
sub = 8
lane = 128
pad = 8
MESH = pl.DeviceIdType.MESH


def dot(left, right, right_dim, left_dim=1):
    return lax.dot_general(
        left, right, (((left_dim,), (right_dim,)), ((), ())),
        precision=lax.Precision.HIGHEST, preferred_element_type=jnp.float32,
    )


def split_pieces(row):
    return [row[:, p * lane : (p + 1) * lane] for p in range(row.shape[1] // lane)]


def swap_piece_and_lane(pieces):
    count = len(pieces)
    lanes = lax.broadcasted_iota(jnp.int32, pieces[0].shape, 1)
    bit = 1
    while bit < count:
        upper = (lanes & bit) > 0
        out = list(pieces)
        for p in range(count):
            if p & bit:
                continue
            low, high = pieces[p], pieces[p + bit]
            out[p] = jnp.where(upper, pltpu.roll(high, bit, 1), low)
            out[p + bit] = jnp.where(upper, high, pltpu.roll(low, lane - bit, 1))
        pieces = out
        bit *= 2
    return pieces


def take_lanes(pieces, index):
    return [jnp.take_along_axis(p, index, axis=1, mode="promise_in_bounds") for p in pieces]


def to_strided(row):
    pieces = swap_piece_and_lane(split_pieces(row))
    count = len(pieces)
    lanes = lax.broadcasted_iota(jnp.int32, pieces[0].shape, 1)
    run = lane // count
    shift = run.bit_length() - 1
    return jnp.concatenate(take_lanes(pieces, (lanes & (run - 1)) * count + (lanes >> shift)), axis=1)


def to_natural(row):
    pieces = split_pieces(row)
    count = len(pieces)
    lanes = lax.broadcasted_iota(jnp.int32, pieces[0].shape, 1)
    shift = count.bit_length() - 1
    index = (lanes & (count - 1)) * (lane // count) + (lanes >> shift)
    return jnp.concatenate(swap_piece_and_lane(take_lanes(pieces, index)), axis=1)


def diffuse(h, slip):
    square = h * h
    return (slip * square) * pl.reciprocal(1.0 + square, approx=True)


def sweep(source, target, slip_ref, bal_ref, mask, first, count, turns):
    lanes = lax.broadcasted_iota(jnp.int32, (sub, lane), 1)
    at_end = lanes == lane - 1
    at_start = lanes == 0

    def load(row):
        h = source[pad + row]
        return h, diffuse(h, slip_ref[pad + row])

    def body(turn, carry):
        begin = first + turn * count
        h, d, f_up = carry
        for k in range(count):
            row = begin + k
            h_below, d_below = load(row + 1)
            f_down = (d_below + d) * (h_below - h)
            wrapped_h = jnp.where(at_end, 0.0, pltpu.roll(h[:, :lane], lane - 1, 1))
            wrapped_d = jnp.where(at_end, 0.0, pltpu.roll(d[:, :lane], lane - 1, 1))
            h_next = jnp.concatenate([h[:, lane:], wrapped_h], axis=1)
            d_next = jnp.concatenate([d[:, lane:], wrapped_d], axis=1)
            f_right = (d_next + d) * (h_next - h)
            edge = jnp.where(
                at_start, d[:, :lane] * h[:, :lane], pltpu.roll(f_right[:, -lane:], 1, 1)
            )
            f_left = jnp.concatenate([edge, f_right[:, :-lane]], axis=1)
            change = (f_down - f_up) + (f_right - f_left)
            balance = jnp.broadcast_to(bal_ref[pl.ds(pad + row, 1)], h.shape)
            moved = (h + balance) + change
            target[pad + row] = jnp.where(mask(row), moved, h)
            h, d, f_up = h_below, d_below, f_down
        return h, d, f_up

    h_above, d_above = load(first - 1)
    h, d = load(first)
    carry = (h, d, (d + d_above) * (h - h_above))
    if turns == 1:
        body(0, carry)
    else:
        lax.fori_loop(0, turns, body, carry)


def kernel(
    spaces, enss, params_ref, base_hbm, balance_hbm, count_hbm, index_hbm, observed_hbm, noise_hbm,
    out_ref, parts_ref, weights_ref, own_ref,
    count_ref, observed_ref, noise_ref, raw_ref, par_ref, bb_ref, index_land, even_ref, odd_ref, slip_ref, base_c, bal_c, land_ref, sent_ref,
    one_hot_ref, pick_ref, pred_ref, stage_ref, turned_ref, sum_ref, sum_land,
    raw_send, raw_recv, bb_send, bb_recv, index_send, index_recv, ens_send, ens_recv, local_sem,
    edge_send, edge_recv, h_send, h_recv, pred_send, pred_recv, thick_send, thick_recv,
    sum_send, sum_recv,
):
    rows, width = base_hbm.shape
    members = params_ref.shape[0]
    quad = members // sub
    groups = quad * enss
    total = quad * rows
    every = members * enss
    blocks = steps // halo
    count_obs = index_hbm.shape[1]
    pieces = width // lane

    me = lax.axis_index("space")
    ens = lax.axis_index("ens")
    pos = lax.rem(me, quad)
    home = me - pos
    has_up = home > 0
    has_down = home + quad < spaces
    up = jnp.maximum(me - quad, 0)
    down = jnp.minimum(me + quad, spaces - 1)
    sides = ((has_up, up, 1), (has_down, down, 0))

    twin = pos + 1 - 2 * lax.rem(pos, 2)
    far = [lax.rem(pos + 2, quad), lax.rem(twin + 2, quad)] if quad > 2 else []
    mates = far + [twin] * (quad > 1)
    others = [lax.rem(ens + d, enss) for d in range(1, enss)]
    peers = [
        (lax.rem(pos + d, quad), lax.rem(ens + e, enss))
        for d in range(quad) for e in range(enss) if d or e
    ]
    stages = spaces.bit_length() - 1
    inner = quad.bit_length() - 1
    bits = [0] + list(range(max(inner, 1), stages)) + list(range(1, inner))
    bits = bits[:stages]
    partners = []
    for stage in bits:
        bit = 1 << stage
        partners.append(me + bit - 2 * bit * lax.rem(lax.div(me, bit), 2))

    fetches = [
        pltpu.make_async_copy(source, dest, local_sem.at[k])
        for k, (source, dest) in enumerate((
            (params_ref.at[pl.ds(pos * sub, sub)], raw_ref.at[pos]),
            (base_hbm, bb_ref.at[0, pos]),
            (balance_hbm, bb_ref.at[1, pos]),
            (count_hbm, count_ref),
            (index_hbm, index_land.at[pos]),
            (observed_hbm, observed_ref),
            (noise_hbm, noise_ref),
            (params_ref, own_ref),
            (params_ref, par_ref.at[ens]),
        ))
    ]
    own_raw, own_params = fetches[0], fetches[-1]
    barrier = pltpu.get_barrier_semaphore()
    for mate, other in peers:
        pl.semaphore_signal(
            barrier, inc=1, device_id={"space": home + mate, "ens": other}, device_id_type=MESH
        )
    for have, target, _ in sides:
        @pl.when(have)
        def _(target=target):
            pl.semaphore_signal(barrier, inc=1, device_id={"space": target}, device_id_type=MESH)
    outer = [partner for bit, partner in zip(bits, partners) if bit >= inner]
    for partner in outer:
        pl.semaphore_signal(barrier, inc=1, device_id={"space": partner}, device_id_type=MESH)
    for fetch in fetches:
        fetch.start()
    pl.semaphore_wait(
        barrier, len(peers) + len(outer) + has_up.astype(jnp.int32) + has_down.astype(jnp.int32)
    )

    def raw_copy(mate, source, slot):
        return pltpu.make_async_remote_copy(
            params_ref.at[pl.ds(mate * sub, sub)], raw_ref.at[source],
            raw_send.at[slot], raw_recv.at[source],
            device_id={"space": home + mate}, device_id_type=MESH,
        )

    def bb_copy(which, mate, source, slot, passed=False):
        ref = bb_ref.at[which, source] if passed else (base_hbm, balance_hbm)[which]
        return pltpu.make_async_remote_copy(
            ref, bb_ref.at[which, source], bb_send.at[which, slot], bb_recv.at[which, source],
            device_id={"space": home + mate}, device_id_type=MESH,
        )

    def index_copy(mate, source, slot):
        return pltpu.make_async_remote_copy(
            index_hbm, index_land.at[source], index_send.at[slot], index_recv.at[source],
            device_id={"space": home + mate}, device_id_type=MESH,
        )

    def ens_copy(step, source):
        return pltpu.make_async_remote_copy(
            params_ref, par_ref.at[source], ens_send.at[step], ens_recv.at[source],
            device_id={"ens": others[step]}, device_id_type=MESH,
        )

    for slot, mate in enumerate(mates):
        if slot != 1:
            for which in range(2):
                bb_copy(which, mate, pos, slot).start()
        raw_copy(mate, pos, slot).start()
    for slot, mate in enumerate(mates):
        index_copy(mate, pos, slot).start()
    for step in range(enss - 1):
        ens_copy(step, ens).start()

    for fetch in fetches[1:-2]:
        fetch.wait()
    counts = count_ref[...].astype(jnp.float32)
    first_member = ens * members + pos * sub
    mine = (
        lax.broadcasted_iota(jnp.int32, (sub, every), 1)
        == lax.broadcasted_iota(jnp.int32, (sub, every), 0) + first_member
    )
    count = jnp.broadcast_to(
        jnp.sum(jnp.where(mine, jnp.broadcast_to(counts, (sub, every)), 0.0), axis=1, keepdims=True),
        (sub, lane),
    )

    zero = jnp.zeros((sub, width), jnp.float32)
    for side, (have, _, _) in enumerate(sides):
        begin = pad - halo if side == 0 else pad + total

        @pl.when(jnp.logical_not(have))
        def _(side=side, begin=begin):
            for row in range(halo):
                slip_ref[begin + row] = zero
                even_ref[begin + row] = zero
                odd_ref[begin + row] = zero
            edge = 0 if side == 0 else pad + total
            base_c[pl.ds(edge, pad)] = zero
            bal_c[pl.ds(edge, pad)] = zero

    def use_bb(source):
        @pl.loop(0, rows // sub)
        def _(tile):
            at = pl.multiple_of(tile * sub, sub)
            to = pl.multiple_of(pad + source * rows + at, sub)
            base_c[pl.ds(to, sub)] = to_strided(bb_ref[0, source, pl.ds(at, sub)])
            bal_c[pl.ds(to, sub)] = to_strided(bb_ref[1, source, pl.ds(at, sub)] * time_step)

        @pl.loop(0, rows)
        def _(row):
            at = source * rows + row + pad
            even_ref[at] = jnp.broadcast_to(base_c[pl.ds(at, 1)], (sub, width))

    def use_raw(source):
        @pl.loop(0, rows // sub)
        def _(tile):
            at = pl.multiple_of(tile * sub, sub)
            turned = jnp.swapaxes(raw_ref[source, :, pl.ds(at, sub)], 0, 1)
            slip = (jnp.exp(turned) * (0.5 * time_step)).reshape(sub * sub, width)
            slip_ref[pl.ds(pad + source * rows + at, sub)] = to_strided(slip).reshape(sub, sub, width)

    use_bb(pos)
    own_raw.wait()
    use_raw(pos)
    for slot, mate in enumerate(mates):
        for which in range(2):
            bb_copy(which, mate, mate, 0).wait_recv()
            if far and slot == 0:
                bb_copy(which, twin, mate, 1, True).start()
    for mate in mates:
        use_bb(mate)
    for mate in mates:
        index_copy(mate, mate, 0).wait_recv()

    shift = width.bit_length() - 1
    turn = pieces.bit_length() - 1

    def place_of(source):
        index = index_land[source]
        column = index & (width - 1)
        return index >> shift, (column & (pieces - 1)) * lane + (column >> turn)

    @pl.loop(0, quad)
    def _(source):
        _, place = place_of(source)
        one_hot_ref[source] = jnp.where(
            lax.broadcasted_iota(jnp.int32, (width, count_obs), 0) == place, 1.0, 0.0
        ).astype(jnp.bfloat16)

    for mate in reversed(mates):
        raw_copy(mate, mate, 0).wait_recv()
        use_raw(mate)

    def edge_copies(side):
        _, target, there = sides[side]
        slip_from = pad if side == 0 else pad + total - halo
        slip_to = pad + total if side == 0 else pad - halo
        row_from = pad if side == 0 else total
        row_to = pad + total if side == 0 else 0
        pairs = (
            (slip_ref.at[pl.ds(slip_from, halo)], slip_ref.at[pl.ds(slip_to, halo)]),
            (base_c.at[pl.ds(row_from, pad)], base_c.at[pl.ds(row_to, pad)]),
            (bal_c.at[pl.ds(row_from, pad)], bal_c.at[pl.ds(row_to, pad)]),
        )
        return [
            pltpu.make_async_remote_copy(
                source, dest, edge_send.at[side, k], edge_recv.at[there, k],
                device_id={"space": target}, device_id_type=MESH,
            )
            for k, (source, dest) in enumerate(pairs)
        ]

    def edge_arrivals(side):
        _, target, _ = sides[side]
        slip_at = pad - halo if side == 0 else pad + total
        row_at = 0 if side == 0 else pad + total
        refs = (
            slip_ref.at[pl.ds(slip_at, halo)], base_c.at[pl.ds(row_at, pad)],
            bal_c.at[pl.ds(row_at, pad)],
        )
        return [
            pltpu.make_async_remote_copy(
                ref, ref, edge_send.at[side, k], edge_recv.at[side, k],
                device_id={"space": target}, device_id_type=MESH,
            )
            for k, ref in enumerate(refs)
        ]

    for side in range(2):
        @pl.when(sides[side][0])
        def _(side=side):
            for copy in edge_copies(side):
                copy.start()

    def h_copy(side, slot):
        _, target, there = sides[side]
        return pltpu.make_async_remote_copy(
            sent_ref.at[slot, side], land_ref.at[slot, there],
            h_send.at[slot, side], h_recv.at[slot, there],
            device_id={"space": target}, device_id_type=MESH,
        )

    def h_arrival(side, slot):
        _, target, _ = sides[side]
        return pltpu.make_async_remote_copy(
            sent_ref.at[slot, side], land_ref.at[slot, side],
            h_send.at[slot, side], h_recv.at[slot, side],
            device_id={"space": target}, device_id_type=MESH,
        )

    beyond = (count * has_up.astype(jnp.float32), count * has_down.astype(jnp.float32))

    @pl.loop(0, blocks)
    def _(block):
        slot = lax.rem(block, 2)
        begin = (block * halo).astype(jnp.float32)
        buffers = (even_ref, odd_ref)

        def wide(mask):
            return jnp.concatenate([mask] * pieces, axis=1)

        for level in range(1, halo + 1):
            active = wide((begin + float(level - 1)) < count)
            sweep(
                buffers[(level - 1) % 2], buffers[level % 2], slip_ref, bal_c,
                lambda row: active, level, total // 2 - level, 2,
            )

        for side in range(2):
            at = pad - halo if side == 0 else pad + total

            @pl.when(jnp.logical_and(sides[side][0], block == 0))
            def _(side=side, at=at):
                for copy in edge_arrivals(side):
                    copy.wait_recv()
                for row in range(halo):
                    even_ref[at + row] = jnp.broadcast_to(base_c[pl.ds(at + row, 1)], (sub, width))

            @pl.when(jnp.logical_and(sides[side][0], block > 0))
            def _(side=side, at=at):
                h_arrival(side, slot).wait_recv()
                even_ref[pl.ds(at, halo)] = land_ref[slot, side]

            @pl.when(jnp.logical_and(sides[side][0], block > 1))
            def _(side=side):
                h_copy(side, 1 - slot).wait_send()

        @pl.loop(0, halo // 2)
        def _(pair):
            for odd in range(2):
                level = pair * 2 + (odd + 1)
                now = begin + (level - 1).astype(jnp.float32)
                for side in range(2):
                    first = level - halo if side == 0 else total - level

                    def mask(row, side=side, now=now):
                        outside = row < 0 if side == 0 else row >= total
                        return wide(now < jnp.where(outside, beyond[side], count))

                    sweep(
                        buffers[odd], buffers[1 - odd], slip_ref, bal_c, mask, first, halo, 1
                    )

        for side in range(2):
            at = pad if side == 0 else pad + total - halo
            sent_ref[1 - slot, side] = even_ref[pl.ds(at, halo)]

        for side in range(2):
            @pl.when(jnp.logical_and(sides[side][0], block < blocks - 1))
            def _(side=side):
                h_copy(side, 1 - slot).start()

    for source in range(quad):
        cells = even_ref[pl.ds(pad + source * rows, rows)].reshape(rows * sub, width)
        picked = None
        one_hot = one_hot_ref[source]
        for part in range(3):
            cut = cells.astype(jnp.bfloat16)
            if part < 2:
                cells = cells - cut.astype(jnp.float32)
            term = jnp.dot(cut, one_hot, preferred_element_type=jnp.float32)
            picked = term if picked is None else picked + term
        row_at, _ = place_of(source)
        at_row = lax.broadcasted_iota(jnp.int32, (rows, sub, count_obs), 0) == row_at
        pick_ref[source] = jnp.sum(
            jnp.where(at_row, picked.reshape(rows, sub, count_obs), 0.0), axis=0
        )

    def pred_copy(k, source_ens, source_pos):
        mate, other = peers[k]
        return pltpu.make_async_remote_copy(
            pick_ref.at[mate], pred_ref.at[source_ens, source_pos],
            pred_send.at[k], pred_recv.at[source_ens, source_pos],
            device_id={"space": home + mate, "ens": other}, device_id_type=MESH,
        )

    for k in range(len(peers)):
        pred_copy(k, ens, pos).start()
    pred_ref[ens, pos] = pick_ref[pos]

    def thick_copy(mate, source, slot):
        return pltpu.make_async_remote_copy(
            stage_ref.at[mate], out_ref.at[pl.ds(source * sub, sub)],
            thick_send.at[slot], thick_recv.at[source],
            device_id={"space": home + mate}, device_id_type=MESH,
        )

    def unturn(mate):
        @pl.loop(0, rows // sub)
        def _(tile):
            at = pl.multiple_of(tile * sub, sub)
            cells = even_ref[pl.ds(pad + mate * rows + at, sub)].reshape(sub * sub, width)
            stage_ref[mate, :, pl.ds(at, sub)] = jnp.swapaxes(
                to_natural(cells).reshape(sub, sub, width), 0, 1
            )

    for slot, mate in enumerate(mates):
        unturn(mate)
        thick_copy(mate, pos, slot).start()
    unturn(pos)
    own_thick = pltpu.make_async_copy(
        stage_ref.at[pos], out_ref.at[pl.ds(pos * sub, sub)], local_sem.at[9]
    )
    own_thick.start()
    for k, (mate, other) in enumerate(peers):
        pred_copy(k, other, mate).wait_recv()

    scaling = lax.rsqrt(noise_ref[...])
    predicted = pred_ref[...].reshape(every, count_obs)
    average = jnp.sum(predicted, axis=0, keepdims=True) * (1.0 / every)
    root = jnp.sqrt(jnp.float32(every - 1))
    anomalies = (predicted - average) * (scaling / root)
    surprise = (observed_ref[...] - average) * scaling
    spread = sum_ref.shape[2]
    first = lax.broadcasted_iota(jnp.int32, (spread - every, count_obs), 0) == 0
    lower = jnp.where(first, jnp.broadcast_to(surprise, first.shape), 0.0)
    sum_ref[0] = dot(anomalies, jnp.concatenate([anomalies, lower], axis=0), 1)

    def sum_copy(stage):
        return pltpu.make_async_remote_copy(
            sum_ref.at[stage], sum_land.at[stage], sum_send.at[stage], sum_recv.at[stage],
            device_id={"space": partners[stage]}, device_id_type=MESH,
        )

    for stage in range(stages):
        sum_copy(stage).start()
        if stage == min(1, stages - 1):
            fetches[-2].wait()
            own_params.wait()
            for step in range(enss - 1):
                ens_copy(step, others[step]).wait_recv()

            @pl.loop(0, groups)
            def _(group):
                member = pl.multiple_of(lax.rem(group, quad) * sub, sub)
                turned_ref[group] = jnp.swapaxes(
                    par_ref[lax.div(group, quad), pl.ds(member, sub)], 0, 1
                )

            @pl.loop(0, rows)
            def _(row):
                values = turned_ref[:, row].reshape(every, width)
                middle = jnp.sum(turned_ref[:, row], axis=0)
                middle = jnp.sum(middle, axis=0, keepdims=True) * (1.0 / every)
                deviation = values - middle
                high = deviation.astype(jnp.bfloat16)
                parts_ref[row, pl.ds(0, every)] = high
                parts_ref[row, pl.ds(every, every)] = (
                    deviation - high.astype(jnp.float32)
                ).astype(jnp.bfloat16)

        sum_copy(stage).wait_recv()
        sum_ref[stage + 1] = sum_ref[stage] + sum_land[stage]

    row_of = lax.broadcasted_iota(jnp.int32, (every, spread), 0)
    lane_of = lax.broadcasted_iota(jnp.int32, (every, spread), 1)
    own_unit = (row_of + (every + 1) == lane_of + ens * members) & (lane_of > every)
    unit = (row_of == lane_of) | own_unit
    system = sum_ref[stages] + jnp.where(unit, 1.0, 0.0)
    for pivot in range(0, every, 2):
        left = jnp.broadcast_to(system[:, pivot : pivot + 1], (every, spread))
        right = jnp.broadcast_to(system[:, pivot + 1 : pivot + 2], (every, spread))
        top, low = system[pivot : pivot + 1], system[pivot + 1 : pivot + 2]
        a, c = left[pivot : pivot + 1], left[pivot + 1 : pivot + 2]
        b, d = right[pivot : pivot + 1], right[pivot + 1 : pivot + 2]
        scale = 1.0 / (a * d - b * c)
        new_top = (d * top - b * low) * scale
        new_low = (a * low - c * top) * scale
        rest = system - left * new_top - right * new_low
        system = jnp.where(
            row_of == pivot, new_top, jnp.where(row_of == pivot + 1, new_low, rest)
        )
    gain = system[:, every : every + 1] / root
    weights = system[:, every + 1 : every + 1 + members] + gain
    weights = weights - jnp.where(
        lax.broadcasted_iota(jnp.int32, (every, members), 0)
        == lax.broadcasted_iota(jnp.int32, (every, members), 1) + ens * members, 1.0, 0.0,
    )
    weights = weights.T
    high = weights.astype(jnp.bfloat16)
    low = (weights - high.astype(jnp.float32)).astype(jnp.bfloat16)
    weights_ref[...] = jnp.concatenate([high, high, low, low], axis=1)

    for mate in mates:
        thick_copy(mate, mate, 0).wait_recv()
    own_thick.wait()
    for slot, mate in enumerate(mates):
        for which in range(2):
            if slot == 1:
                bb_copy(which, twin, far[0], slot, True).wait_send()
            else:
                bb_copy(which, mate, pos, slot).wait_send()
        raw_copy(mate, pos, slot).wait_send()
        index_copy(mate, pos, slot).wait_send()
        thick_copy(mate, pos, slot).wait_send()
    for step in range(enss - 1):
        ens_copy(step, ens).wait_send()
    for k in range(len(peers)):
        pred_copy(k, ens, pos).wait_send()
    for stage in range(stages):
        sum_copy(stage).wait_send()
    for side in range(2):
        @pl.when(sides[side][0])
        def _(side=side):
            for copy in edge_copies(side):
                copy.wait_send()
            h_copy(side, (blocks - 1) % 2).wait_send()


def finish_kernel(thick_ref, params_ref, parts_ref, weights_ref, out_ref, updated_ref, made_ref, sem):
    members, rows, width = params_ref.shape
    quad = members // sub
    thick = pltpu.make_async_copy(thick_ref, out_ref, sem.at[0])
    thick.start()
    weights = weights_ref[...]
    copies = []
    for tile in range(rows // sub):
        here = pl.ds(tile * sub, sub)
        steps_made = []
        for k in range(sub):
            part = parts_ref[tile * sub + k]
            steps_made.append(jnp.dot(
                weights, jnp.concatenate([part, part], axis=0), preferred_element_type=jnp.float32
            ))
        for group in range(quad):
            own = slice(group * sub, (group + 1) * sub)
            made = jnp.stack([step[own] for step in steps_made])
            made_ref[pl.ds(group * sub, sub), here] = (
                params_ref[pl.ds(group * sub, sub), here] + jnp.swapaxes(made, 0, 1)
            )
        copies.append(pltpu.make_async_copy(
            made_ref.at[:, here], updated_ref.at[:, here], sem.at[1 + tile]
        ))
        copies[-1].start()
    for copy in copies:
        copy.wait()
    thick.wait()


def shards(params, base_thickness, balance, step_count, obs_index, observed, noise_var):
    members, rows, width = params.shape
    spaces, enss = lax.axis_size("space"), lax.axis_size("ens")
    quad = members // sub
    total = quad * rows
    every = members * enss
    count_obs = obs_index.shape[0]
    spread = pl.cdiv(every + 1 + members, lane) * lane
    stages = spaces.bit_length() - 1
    assert 1 << stages == spaces and spaces % quad == 0 and quad in (1, 2, 4)
    assert width & (width - 1) == 0 and steps // halo > 2
    dma = pltpu.SemaphoreType.DMA
    vmem = pl.BlockSpec(memory_space=pltpu.VMEM)
    f32 = jnp.float32
    many = max(quad - 1, 1)
    flat = jax.ShapeDtypeStruct(params.shape, f32)
    thick, parts, weights, own = pl.pallas_call(
        functools.partial(kernel, spaces, enss),
        out_shape=(
            flat,
            jax.ShapeDtypeStruct((rows, 2 * every, width), jnp.bfloat16),
            jax.ShapeDtypeStruct((members, 4 * every), jnp.bfloat16),
            flat,
        ),
        in_specs=[pl.BlockSpec(memory_space=pltpu.HBM)] * 7,
        out_specs=(vmem,) * 4,
        scratch_shapes=[
            pltpu.VMEM((1, every), jnp.int32),
            pltpu.VMEM((1, count_obs), f32),
            pltpu.VMEM((1, count_obs), f32),
            pltpu.VMEM((quad, sub, rows, width), f32),
            pltpu.VMEM((enss, members, rows, width), f32),
            pltpu.VMEM((2, quad, rows, width), f32),
            pltpu.VMEM((quad, 1, count_obs), jnp.int32),
            pltpu.VMEM((total + 2 * pad, sub, width), f32),
            pltpu.VMEM((total + 2 * pad, sub, width), f32),
            pltpu.VMEM((total + 2 * pad, sub, width), f32),
            pltpu.VMEM((total + 2 * pad, width), f32),
            pltpu.VMEM((total + 2 * pad, width), f32),
            pltpu.VMEM((2, 2, halo, sub, width), f32),
            pltpu.VMEM((2, 2, halo, sub, width), f32),
            pltpu.VMEM((quad, width, count_obs), jnp.bfloat16),
            pltpu.VMEM((quad, sub, count_obs), f32),
            pltpu.VMEM((enss, quad, sub, count_obs), f32),
            pltpu.VMEM((quad, sub, rows, width), f32),
            pltpu.VMEM((quad * enss, rows, sub, width), f32),
            pltpu.VMEM((stages + 1, every, spread), f32),
            pltpu.VMEM((stages, every, spread), f32),
            dma((many,)), dma((quad,)),
            dma((2, many)), dma((2, quad)),
            dma((many,)), dma((quad,)),
            dma((max(enss - 1, 1),)), dma((enss,)),
            dma((10,)),
            dma((2, 3)), dma((2, 3)),
            dma((2, 2)), dma((2, 2)),
            dma((quad * enss,)), dma((enss, quad)),
            dma((many,)), dma((quad,)),
            dma((stages,)), dma((stages,)),
        ],
        compiler_params=pltpu.CompilerParams(
            collective_id=0, has_side_effects=True, vmem_limit_bytes=48 * 1024 * 1024
        ),
        name="advance",
    )(
        *(pltpu.with_memory_space_constraint(x, pltpu.HBM) for x in (
            params, base_thickness, balance, step_count[None],
            obs_index[None], observed[None], noise_var[None],
        ))
    )
    return pl.pallas_call(
        finish_kernel,
        out_shape=(flat, flat),
        in_specs=[vmem] * 4,
        out_specs=(pl.BlockSpec(memory_space=pltpu.HBM),) * 2,
        scratch_shapes=[pltpu.VMEM(params.shape, f32), dma((1 + rows // sub,))],
        compiler_params=pltpu.CompilerParams(vmem_limit_bytes=8 * 1024 * 1024),
        name="finish",
    )(thick, own, parts, weights)


def solution(mesh):
    in_specs = (
        P("ens", "space", None),
        P("space", None),
        P("space", None),
        P(),
        P("space"),
        P("space"),
        P("space"),
    )
    out_specs = (P("ens", "space", None), P("ens", "space", None))
    return jax.shard_map(shards, mesh=mesh, in_specs=in_specs, out_specs=out_specs, check_vma=False)
```

```python
import functools
import jax
import jax.numpy as jnp
from jax import lax
from jax.experimental import pallas as pl
from jax.experimental.pallas import tpu as pltpu
from jax.sharding import PartitionSpec as P

time_step = 0.11
steps = 32
halo = 8
sub = 8
lane = 128
pad = 8
MESH = pl.DeviceIdType.MESH


def dot(left, right, right_dim, left_dim=1):
    return lax.dot_general(
        left, right, (((left_dim,), (right_dim,)), ((), ())),
        precision=lax.Precision.HIGHEST, preferred_element_type=jnp.float32,
    )


def split_pieces(row):
    return [row[:, p * lane : (p + 1) * lane] for p in range(row.shape[1] // lane)]


def swap_piece_and_lane(pieces):
    count = len(pieces)
    lanes = lax.broadcasted_iota(jnp.int32, pieces[0].shape, 1)
    bit = 1
    while bit < count:
        upper = (lanes & bit) > 0
        out = list(pieces)
        for p in range(count):
            if p & bit:
                continue
            low, high = pieces[p], pieces[p + bit]
            out[p] = jnp.where(upper, pltpu.roll(high, bit, 1), low)
            out[p + bit] = jnp.where(upper, high, pltpu.roll(low, lane - bit, 1))
        pieces = out
        bit *= 2
    return pieces


def take_lanes(pieces, index):
    return [jnp.take_along_axis(p, index, axis=1, mode="promise_in_bounds") for p in pieces]


def to_strided(row):
    pieces = swap_piece_and_lane(split_pieces(row))
    count = len(pieces)
    lanes = lax.broadcasted_iota(jnp.int32, pieces[0].shape, 1)
    run = lane // count
    shift = run.bit_length() - 1
    return jnp.concatenate(take_lanes(pieces, (lanes & (run - 1)) * count + (lanes >> shift)), axis=1)


def to_natural(row):
    pieces = split_pieces(row)
    count = len(pieces)
    lanes = lax.broadcasted_iota(jnp.int32, pieces[0].shape, 1)
    shift = count.bit_length() - 1
    index = (lanes & (count - 1)) * (lane // count) + (lanes >> shift)
    return jnp.concatenate(swap_piece_and_lane(take_lanes(pieces, index)), axis=1)


def diffuse(h, slip):
    square = h * h
    return (slip * square) * pl.reciprocal(1.0 + square, approx=True)


def sweep(source, target, slip_ref, bal_ref, mask, first, count, turns):
    lanes = lax.broadcasted_iota(jnp.int32, (sub, lane), 1)
    at_end = lanes == lane - 1
    at_start = lanes == 0

    def load(row):
        h = source[pad + row]
        return h, diffuse(h, slip_ref[pad + row])

    def body(turn, carry):
        begin = first + turn * count
        h, d, f_up = carry
        for k in range(count):
            row = begin + k
            h_below, d_below = load(row + 1)
            f_down = (d_below + d) * (h_below - h)
            wrapped_h = jnp.where(at_end, 0.0, pltpu.roll(h[:, :lane], lane - 1, 1))
            wrapped_d = jnp.where(at_end, 0.0, pltpu.roll(d[:, :lane], lane - 1, 1))
            h_next = jnp.concatenate([h[:, lane:], wrapped_h], axis=1)
            d_next = jnp.concatenate([d[:, lane:], wrapped_d], axis=1)
            f_right = (d_next + d) * (h_next - h)
            edge = jnp.where(
                at_start, d[:, :lane] * h[:, :lane], pltpu.roll(f_right[:, -lane:], 1, 1)
            )
            f_left = jnp.concatenate([edge, f_right[:, :-lane]], axis=1)
            change = (f_down - f_up) + (f_right - f_left)
            balance = jnp.broadcast_to(bal_ref[pl.ds(pad + row, 1)], h.shape)
            moved = (h + balance) + change
            target[pad + row] = jnp.where(mask(row), moved, h)
            h, d, f_up = h_below, d_below, f_down
        return h, d, f_up

    h_above, d_above = load(first - 1)
    h, d = load(first)
    carry = (h, d, (d + d_above) * (h - h_above))
    if turns == 1:
        body(0, carry)
    else:
        lax.fori_loop(0, turns, body, carry)


def kernel(
    spaces, enss, params_ref, base_hbm, balance_hbm, count_hbm, index_hbm, observed_hbm, noise_hbm,
    out_ref, parts_ref, weights_ref, own_ref,
    count_ref, observed_ref, noise_ref, raw_ref, par_ref, bb_ref, index_land, even_ref, odd_ref, slip_ref, base_c, bal_c, land_ref, sent_ref,
    one_hot_ref, pick_ref, pred_ref, stage_ref, turned_ref, sum_ref, sum_land,
    raw_send, raw_recv, bb_send, bb_recv, index_send, index_recv, ens_send, ens_recv, local_sem,
    edge_send, edge_recv, h_send, h_recv, pred_send, pred_recv, thick_send, thick_recv,
    sum_send, sum_recv,
):
    rows, width = base_hbm.shape
    members = params_ref.shape[0]
    quad = members // sub
    groups = quad * enss
    total = quad * rows
    every = members * enss
    blocks = steps // halo
    count_obs = index_hbm.shape[1]
    pieces = width // lane

    me = lax.axis_index("space")
    ens = lax.axis_index("ens")
    pos = lax.rem(me, quad)
    home = me - pos
    has_up = home > 0
    has_down = home + quad < spaces
    up = jnp.maximum(me - quad, 0)
    down = jnp.minimum(me + quad, spaces - 1)
    sides = ((has_up, up, 1), (has_down, down, 0))

    twin = pos + 1 - 2 * lax.rem(pos, 2)
    far = [lax.rem(pos + 2, quad), lax.rem(twin + 2, quad)] if quad > 2 else []
    mates = far + [twin] * (quad > 1)
    others = [lax.rem(ens + d, enss) for d in range(1, enss)]
    peers = [
        (lax.rem(pos + d, quad), lax.rem(ens + e, enss))
        for d in range(quad) for e in range(enss) if d or e
    ]
    stages = spaces.bit_length() - 1
    inner = quad.bit_length() - 1
    bits = [0] + list(range(max(inner, 1), stages)) + list(range(1, inner))
    bits = bits[:stages]
    partners = []
    for stage in bits:
        bit = 1 << stage
        partners.append(me + bit - 2 * bit * lax.rem(lax.div(me, bit), 2))

    fetches = [
        pltpu.make_async_copy(source, dest, local_sem.at[k])
        for k, (source, dest) in enumerate((
            (params_ref.at[pl.ds(pos * sub, sub)], raw_ref.at[pos]),
            (base_hbm, bb_ref.at[0, pos]),
            (balance_hbm, bb_ref.at[1, pos]),
            (count_hbm, count_ref),
            (index_hbm, index_land.at[pos]),
            (observed_hbm, observed_ref),
            (noise_hbm, noise_ref),
            (params_ref, own_ref),
            (params_ref, par_ref.at[ens]),
        ))
    ]
    own_raw, own_params = fetches[0], fetches[-1]
    barrier = pltpu.get_barrier_semaphore()
    for mate, other in peers:
        pl.semaphore_signal(
            barrier, inc=1, device_id={"space": home + mate, "ens": other}, device_id_type=MESH
        )
    for have, target, _ in sides:
        @pl.when(have)
        def _(target=target):
            pl.semaphore_signal(barrier, inc=1, device_id={"space": target}, device_id_type=MESH)
    outer = [partner for bit, partner in zip(bits, partners) if bit >= inner]
    for partner in outer:
        pl.semaphore_signal(barrier, inc=1, device_id={"space": partner}, device_id_type=MESH)
    for fetch in fetches:
        fetch.start()
    pl.semaphore_wait(
        barrier, len(peers) + len(outer) + has_up.astype(jnp.int32) + has_down.astype(jnp.int32)
    )

    def raw_copy(mate, source, slot):
        return pltpu.make_async_remote_copy(
            params_ref.at[pl.ds(mate * sub, sub)], raw_ref.at[source],
            raw_send.at[slot], raw_recv.at[source],
            device_id={"space": home + mate}, device_id_type=MESH,
        )

    def bb_copy(which, mate, source, slot, passed=False):
        ref = bb_ref.at[which, source] if passed else (base_hbm, balance_hbm)[which]
        return pltpu.make_async_remote_copy(
            ref, bb_ref.at[which, source], bb_send.at[which, slot], bb_recv.at[which, source],
            device_id={"space": home + mate}, device_id_type=MESH,
        )

    def index_copy(mate, source, slot):
        return pltpu.make_async_remote_copy(
            index_hbm, index_land.at[source], index_send.at[slot], index_recv.at[source],
            device_id={"space": home + mate}, device_id_type=MESH,
        )

    def ens_copy(step, source):
        return pltpu.make_async_remote_copy(
            params_ref, par_ref.at[source], ens_send.at[step], ens_recv.at[source],
            device_id={"ens": others[step]}, device_id_type=MESH,
        )

    for slot, mate in enumerate(mates):
        if slot != 1:
            for which in range(2):
                bb_copy(which, mate, pos, slot).start()
        raw_copy(mate, pos, slot).start()
    for slot, mate in enumerate(mates):
        index_copy(mate, pos, slot).start()
    for step in range(enss - 1):
        ens_copy(step, ens).start()

    for fetch in fetches[1:-2]:
        fetch.wait()
    counts = count_ref[...].astype(jnp.float32)
    first_member = ens * members + pos * sub
    mine = (
        lax.broadcasted_iota(jnp.int32, (sub, every), 1)
        == lax.broadcasted_iota(jnp.int32, (sub, every), 0) + first_member
    )
    count = jnp.broadcast_to(
        jnp.sum(jnp.where(mine, jnp.broadcast_to(counts, (sub, every)), 0.0), axis=1, keepdims=True),
        (sub, lane),
    )

    zero = jnp.zeros((sub, width), jnp.float32)
    for side, (have, _, _) in enumerate(sides):
        begin = pad - halo if side == 0 else pad + total

        @pl.when(jnp.logical_not(have))
        def _(side=side, begin=begin):
            for row in range(halo):
                slip_ref[begin + row] = zero
                even_ref[begin + row] = zero
                odd_ref[begin + row] = zero
            edge = 0 if side == 0 else pad + total
            base_c[pl.ds(edge, pad)] = zero
            bal_c[pl.ds(edge, pad)] = zero

    def use_bb(source):
        @pl.loop(0, rows // sub)
        def _(tile):
            at = pl.multiple_of(tile * sub, sub)
            to = pl.multiple_of(pad + source * rows + at, sub)
            base_c[pl.ds(to, sub)] = to_strided(bb_ref[0, source, pl.ds(at, sub)])
            bal_c[pl.ds(to, sub)] = to_strided(bb_ref[1, source, pl.ds(at, sub)] * time_step)

        @pl.loop(0, rows)
        def _(row):
            at = source * rows + row + pad
            even_ref[at] = jnp.broadcast_to(base_c[pl.ds(at, 1)], (sub, width))

    def use_raw(source):
        @pl.loop(0, rows // sub)
        def _(tile):
            at = pl.multiple_of(tile * sub, sub)
            turned = jnp.swapaxes(raw_ref[source, :, pl.ds(at, sub)], 0, 1)
            slip = (jnp.exp(turned) * (0.5 * time_step)).reshape(sub * sub, width)
            slip_ref[pl.ds(pad + source * rows + at, sub)] = to_strided(slip).reshape(sub, sub, width)

    use_bb(pos)
    own_raw.wait()
    use_raw(pos)
    for slot, mate in enumerate(mates):
        for which in range(2):
            bb_copy(which, mate, mate, 0).wait_recv()
            if far and slot == 0:
                bb_copy(which, twin, mate, 1, True).start()
    for mate in mates:
        use_bb(mate)
    for mate in mates:
        index_copy(mate, mate, 0).wait_recv()

    shift = width.bit_length() - 1
    turn = pieces.bit_length() - 1

    def place_of(source):
        index = index_land[source]
        column = index & (width - 1)
        return index >> shift, (column & (pieces - 1)) * lane + (column >> turn)

    @pl.loop(0, quad)
    def _(source):
        _, place = place_of(source)
        one_hot_ref[source] = jnp.where(
            lax.broadcasted_iota(jnp.int32, (width, count_obs), 0) == place, 1.0, 0.0
        ).astype(jnp.bfloat16)

    for mate in reversed(mates):
        raw_copy(mate, mate, 0).wait_recv()
        use_raw(mate)

    def edge_copies(side):
        _, target, there = sides[side]
        slip_from = pad if side == 0 else pad + total - halo
        slip_to = pad + total if side == 0 else pad - halo
        row_from = pad if side == 0 else total
        row_to = pad + total if side == 0 else 0
        pairs = (
            (slip_ref.at[pl.ds(slip_from, halo)], slip_ref.at[pl.ds(slip_to, halo)]),
            (base_c.at[pl.ds(row_from, pad)], base_c.at[pl.ds(row_to, pad)]),
            (bal_c.at[pl.ds(row_from, pad)], bal_c.at[pl.ds(row_to, pad)]),
        )
        return [
            pltpu.make_async_remote_copy(
                source, dest, edge_send.at[side, k], edge_recv.at[there, k],
                device_id={"space": target}, device_id_type=MESH,
            )
            for k, (source, dest) in enumerate(pairs)
        ]

    def edge_arrivals(side):
        _, target, _ = sides[side]
        slip_at = pad - halo if side == 0 else pad + total
        row_at = 0 if side == 0 else pad + total
        refs = (
            slip_ref.at[pl.ds(slip_at, halo)], base_c.at[pl.ds(row_at, pad)],
            bal_c.at[pl.ds(row_at, pad)],
        )
        return [
            pltpu.make_async_remote_copy(
                ref, ref, edge_send.at[side, k], edge_recv.at[side, k],
                device_id={"space": target}, device_id_type=MESH,
            )
            for k, ref in enumerate(refs)
        ]

    for side in range(2):
        @pl.when(sides[side][0])
        def _(side=side):
            for copy in edge_copies(side):
                copy.start()

    def h_copy(side, slot):
        _, target, there = sides[side]
        return pltpu.make_async_remote_copy(
            sent_ref.at[slot, side], land_ref.at[slot, there],
            h_send.at[slot, side], h_recv.at[slot, there],
            device_id={"space": target}, device_id_type=MESH,
        )

    def h_arrival(side, slot):
        _, target, _ = sides[side]
        return pltpu.make_async_remote_copy(
            sent_ref.at[slot, side], land_ref.at[slot, side],
            h_send.at[slot, side], h_recv.at[slot, side],
            device_id={"space": target}, device_id_type=MESH,
        )

    beyond = (count * has_up.astype(jnp.float32), count * has_down.astype(jnp.float32))

    @pl.loop(0, blocks)
    def _(block):
        slot = lax.rem(block, 2)
        begin = (block * halo).astype(jnp.float32)
        buffers = (even_ref, odd_ref)

        def wide(mask):
            return jnp.concatenate([mask] * pieces, axis=1)

        for level in range(1, halo + 1):
            active = wide((begin + float(level - 1)) < count)
            sweep(
                buffers[(level - 1) % 2], buffers[level % 2], slip_ref, bal_c,
                lambda row: active, level, total // 2 - level, 2,
            )

        for side in range(2):
            at = pad - halo if side == 0 else pad + total

            @pl.when(jnp.logical_and(sides[side][0], block == 0))
            def _(side=side, at=at):
                for copy in edge_arrivals(side):
                    copy.wait_recv()
                for row in range(halo):
                    even_ref[at + row] = jnp.broadcast_to(base_c[pl.ds(at + row, 1)], (sub, width))

            @pl.when(jnp.logical_and(sides[side][0], block > 0))
            def _(side=side, at=at):
                h_arrival(side, slot).wait_recv()
                even_ref[pl.ds(at, halo)] = land_ref[slot, side]

            @pl.when(jnp.logical_and(sides[side][0], block > 1))
            def _(side=side):
                h_copy(side, 1 - slot).wait_send()

        @pl.loop(0, halo // 2)
        def _(pair):
            for odd in range(2):
                level = pair * 2 + (odd + 1)
                now = begin + (level - 1).astype(jnp.float32)
                for side in range(2):
                    first = level - halo if side == 0 else total - level

                    def mask(row, side=side, now=now):
                        outside = row < 0 if side == 0 else row >= total
                        return wide(now < jnp.where(outside, beyond[side], count))

                    sweep(
                        buffers[odd], buffers[1 - odd], slip_ref, bal_c, mask, first, halo, 1
                    )

        for side in range(2):
            at = pad if side == 0 else pad + total - halo
            sent_ref[1 - slot, side] = even_ref[pl.ds(at, halo)]

        for side in range(2):
            @pl.when(jnp.logical_and(sides[side][0], block < blocks - 1))
            def _(side=side):
                h_copy(side, 1 - slot).start()

    for source in range(quad):
        cells = even_ref[pl.ds(pad + source * rows, rows)].reshape(rows * sub, width)
        picked = None
        one_hot = one_hot_ref[source]
        for part in range(3):
            cut = cells.astype(jnp.bfloat16)
            if part < 2:
                cells = cells - cut.astype(jnp.float32)
            term = jnp.dot(cut, one_hot, preferred_element_type=jnp.float32)
            picked = term if picked is None else picked + term
        row_at, _ = place_of(source)
        at_row = lax.broadcasted_iota(jnp.int32, (rows, sub, count_obs), 0) == row_at
        pick_ref[source] = jnp.sum(
            jnp.where(at_row, picked.reshape(rows, sub, count_obs), 0.0), axis=0
        )

    def pred_copy(k, source_ens, source_pos):
        mate, other = peers[k]
        return pltpu.make_async_remote_copy(
            pick_ref.at[mate], pred_ref.at[source_ens, source_pos],
            pred_send.at[k], pred_recv.at[source_ens, source_pos],
            device_id={"space": home + mate, "ens": other}, device_id_type=MESH,
        )

    for k in range(len(peers)):
        pred_copy(k, ens, pos).start()
    pred_ref[ens, pos] = pick_ref[pos]

    def thick_copy(mate, source, slot):
        return pltpu.make_async_remote_copy(
            stage_ref.at[mate], out_ref.at[pl.ds(source * sub, sub)],
            thick_send.at[slot], thick_recv.at[source],
            device_id={"space": home + mate}, device_id_type=MESH,
        )

    def unturn(mate):
        @pl.loop(0, rows // sub)
        def _(tile):
            at = pl.multiple_of(tile * sub, sub)
            cells = even_ref[pl.ds(pad + mate * rows + at, sub)].reshape(sub * sub, width)
            stage_ref[mate, :, pl.ds(at, sub)] = jnp.swapaxes(
                to_natural(cells).reshape(sub, sub, width), 0, 1
            )

    for slot, mate in enumerate(mates):
        unturn(mate)
        thick_copy(mate, pos, slot).start()
    unturn(pos)
    own_thick = pltpu.make_async_copy(
        stage_ref.at[pos], out_ref.at[pl.ds(pos * sub, sub)], local_sem.at[9]
    )
    own_thick.start()
    for k, (mate, other) in enumerate(peers):
        pred_copy(k, other, mate).wait_recv()

    scaling = lax.rsqrt(noise_ref[...])
    predicted = pred_ref[...].reshape(every, count_obs)
    average = jnp.sum(predicted, axis=0, keepdims=True) * (1.0 / every)
    root = jnp.sqrt(jnp.float32(every - 1))
    anomalies = (predicted - average) * (scaling / root)
    surprise = (observed_ref[...] - average) * scaling
    spread = sum_ref.shape[2]
    first = lax.broadcasted_iota(jnp.int32, (spread - every, count_obs), 0) == 0
    lower = jnp.where(first, jnp.broadcast_to(surprise, first.shape), 0.0)
    sum_ref[0] = dot(anomalies, jnp.concatenate([anomalies, lower], axis=0), 1)

    def sum_copy(stage):
        return pltpu.make_async_remote_copy(
            sum_ref.at[stage], sum_land.at[stage], sum_send.at[stage], sum_recv.at[stage],
            device_id={"space": partners[stage]}, device_id_type=MESH,
        )

    for stage in range(stages):
        sum_copy(stage).start()
        if stage == min(1, stages - 1):
            fetches[-2].wait()
            own_params.wait()
            for step in range(enss - 1):
                ens_copy(step, others[step]).wait_recv()

            @pl.loop(0, groups)
            def _(group):
                member = pl.multiple_of(lax.rem(group, quad) * sub, sub)
                turned_ref[group] = jnp.swapaxes(
                    par_ref[lax.div(group, quad), pl.ds(member, sub)], 0, 1
                )

            @pl.loop(0, rows)
            def _(row):
                values = turned_ref[:, row].reshape(every, width)
                middle = jnp.sum(turned_ref[:, row], axis=0)
                middle = jnp.sum(middle, axis=0, keepdims=True) * (1.0 / every)
                deviation = values - middle
                high = deviation.astype(jnp.bfloat16)
                parts_ref[row, pl.ds(0, every)] = high
                parts_ref[row, pl.ds(every, every)] = (
                    deviation - high.astype(jnp.float32)
                ).astype(jnp.bfloat16)

        sum_copy(stage).wait_recv()
        sum_ref[stage + 1] = sum_ref[stage] + sum_land[stage]

    row_of = lax.broadcasted_iota(jnp.int32, (every, spread), 0)
    lane_of = lax.broadcasted_iota(jnp.int32, (every, spread), 1)
    own_unit = (row_of + (every + 1) == lane_of + ens * members) & (lane_of > every)
    unit = (row_of == lane_of) | own_unit
    system = sum_ref[stages] + jnp.where(unit, 1.0, 0.0)
    for pivot in range(0, every, 4):
        four = range(4)
        columns = [
            jnp.broadcast_to(system[:, pivot + k : pivot + k + 1], (every, spread)) for k in four
        ]
        lines = [system[pivot + k : pivot + k + 1] for k in four]
        m = [[columns[j][pivot + i : pivot + i + 1] for j in four] for i in four]
        scale = 1.0 / (m[0][0] * m[1][1] - m[0][1] * m[1][0])

        def first_pair(x, y, m=m, scale=scale):
            return (m[1][1] * x - m[0][1] * y) * scale, (m[0][0] * y - m[1][0] * x) * scale

        b = [first_pair(m[0][k], m[1][k]) for k in (2, 3)]
        new = list(first_pair(lines[0], lines[1]))
        d = [[m[i][2 + k] - m[i][0] * b[k][0] - m[i][1] * b[k][1] for k in (0, 1)] for i in (2, 3)]
        y = [lines[i] - m[i][0] * new[0] - m[i][1] * new[1] for i in (2, 3)]
        scale = 1.0 / (d[0][0] * d[1][1] - d[0][1] * d[1][0])
        new.append((d[1][1] * y[0] - d[0][1] * y[1]) * scale)
        new.append((d[0][0] * y[1] - d[1][0] * y[0]) * scale)
        for i in (0, 1):
            new[i] = new[i] - b[0][i] * new[2] - b[1][i] * new[3]
        rest = system
        for k in four:
            rest = rest - columns[k] * new[k]
        for k in four:
            rest = jnp.where(row_of == pivot + k, new[k], rest)
        system = rest
    gain = system[:, every : every + 1] / root
    weights = system[:, every + 1 : every + 1 + members] + gain
    weights = weights - jnp.where(
        lax.broadcasted_iota(jnp.int32, (every, members), 0)
        == lax.broadcasted_iota(jnp.int32, (every, members), 1) + ens * members, 1.0, 0.0,
    )
    weights = weights.T
    high = weights.astype(jnp.bfloat16)
    low = (weights - high.astype(jnp.float32)).astype(jnp.bfloat16)
    weights_ref[...] = jnp.concatenate([high, high, low, low], axis=1)

    for mate in mates:
        thick_copy(mate, mate, 0).wait_recv()
    own_thick.wait()
    for slot, mate in enumerate(mates):
        for which in range(2):
            if slot == 1:
                bb_copy(which, twin, far[0], slot, True).wait_send()
            else:
                bb_copy(which, mate, pos, slot).wait_send()
        raw_copy(mate, pos, slot).wait_send()
        index_copy(mate, pos, slot).wait_send()
        thick_copy(mate, pos, slot).wait_send()
    for step in range(enss - 1):
        ens_copy(step, ens).wait_send()
    for k in range(len(peers)):
        pred_copy(k, ens, pos).wait_send()
    for stage in range(stages):
        sum_copy(stage).wait_send()
    for side in range(2):
        @pl.when(sides[side][0])
        def _(side=side):
            for copy in edge_copies(side):
                copy.wait_send()
            h_copy(side, (blocks - 1) % 2).wait_send()


def finish_kernel(thick_ref, params_ref, parts_ref, weights_ref, out_ref, updated_ref, made_ref, sem):
    members, rows, width = params_ref.shape
    quad = members // sub
    thick = pltpu.make_async_copy(thick_ref, out_ref, sem.at[0])
    thick.start()
    weights = weights_ref[...]
    copies = []
    for tile in range(rows // sub):
        here = pl.ds(tile * sub, sub)
        steps_made = []
        for k in range(sub):
            part = parts_ref[tile * sub + k]
            steps_made.append(jnp.dot(
                weights, jnp.concatenate([part, part], axis=0), preferred_element_type=jnp.float32
            ))
        for group in range(quad):
            own = slice(group * sub, (group + 1) * sub)
            made = jnp.stack([step[own] for step in steps_made])
            made_ref[pl.ds(group * sub, sub), here] = (
                params_ref[pl.ds(group * sub, sub), here] + jnp.swapaxes(made, 0, 1)
            )
        copies.append(pltpu.make_async_copy(
            made_ref.at[:, here], updated_ref.at[:, here], sem.at[1 + tile]
        ))
        copies[-1].start()
    for copy in copies:
        copy.wait()
    thick.wait()


def shards(params, base_thickness, balance, step_count, obs_index, observed, noise_var):
    members, rows, width = params.shape
    spaces, enss = lax.axis_size("space"), lax.axis_size("ens")
    quad = members // sub
    total = quad * rows
    every = members * enss
    count_obs = obs_index.shape[0]
    spread = pl.cdiv(every + 1 + members, lane) * lane
    stages = spaces.bit_length() - 1
    assert 1 << stages == spaces and spaces % quad == 0 and quad in (1, 2, 4)
    assert width & (width - 1) == 0 and steps // halo > 2
    dma = pltpu.SemaphoreType.DMA
    vmem = pl.BlockSpec(memory_space=pltpu.VMEM)
    f32 = jnp.float32
    many = max(quad - 1, 1)
    flat = jax.ShapeDtypeStruct(params.shape, f32)
    thick, parts, weights, own = pl.pallas_call(
        functools.partial(kernel, spaces, enss),
        out_shape=(
            flat,
            jax.ShapeDtypeStruct((rows, 2 * every, width), jnp.bfloat16),
            jax.ShapeDtypeStruct((members, 4 * every), jnp.bfloat16),
            flat,
        ),
        in_specs=[pl.BlockSpec(memory_space=pltpu.HBM)] * 7,
        out_specs=(vmem,) * 4,
        scratch_shapes=[
            pltpu.VMEM((1, every), jnp.int32),
            pltpu.VMEM((1, count_obs), f32),
            pltpu.VMEM((1, count_obs), f32),
            pltpu.VMEM((quad, sub, rows, width), f32),
            pltpu.VMEM((enss, members, rows, width), f32),
            pltpu.VMEM((2, quad, rows, width), f32),
            pltpu.VMEM((quad, 1, count_obs), jnp.int32),
            pltpu.VMEM((total + 2 * pad, sub, width), f32),
            pltpu.VMEM((total + 2 * pad, sub, width), f32),
            pltpu.VMEM((total + 2 * pad, sub, width), f32),
            pltpu.VMEM((total + 2 * pad, width), f32),
            pltpu.VMEM((total + 2 * pad, width), f32),
            pltpu.VMEM((2, 2, halo, sub, width), f32),
            pltpu.VMEM((2, 2, halo, sub, width), f32),
            pltpu.VMEM((quad, width, count_obs), jnp.bfloat16),
            pltpu.VMEM((quad, sub, count_obs), f32),
            pltpu.VMEM((enss, quad, sub, count_obs), f32),
            pltpu.VMEM((quad, sub, rows, width), f32),
            pltpu.VMEM((quad * enss, rows, sub, width), f32),
            pltpu.VMEM((stages + 1, every, spread), f32),
            pltpu.VMEM((stages, every, spread), f32),
            dma((many,)), dma((quad,)),
            dma((2, many)), dma((2, quad)),
            dma((many,)), dma((quad,)),
            dma((max(enss - 1, 1),)), dma((enss,)),
            dma((10,)),
            dma((2, 3)), dma((2, 3)),
            dma((2, 2)), dma((2, 2)),
            dma((quad * enss,)), dma((enss, quad)),
            dma((many,)), dma((quad,)),
            dma((stages,)), dma((stages,)),
        ],
        compiler_params=pltpu.CompilerParams(
            collective_id=0, has_side_effects=True, vmem_limit_bytes=48 * 1024 * 1024
        ),
        name="advance",
    )(
        *(pltpu.with_memory_space_constraint(x, pltpu.HBM) for x in (
            params, base_thickness, balance, step_count[None],
            obs_index[None], observed[None], noise_var[None],
        ))
    )
    return pl.pallas_call(
        finish_kernel,
        out_shape=(flat, flat),
        in_specs=[vmem] * 4,
        out_specs=(pl.BlockSpec(memory_space=pltpu.HBM),) * 2,
        scratch_shapes=[pltpu.VMEM(params.shape, f32), dma((1 + rows // sub,))],
        compiler_params=pltpu.CompilerParams(vmem_limit_bytes=8 * 1024 * 1024),
        name="finish",
    )(thick, own, parts, weights)


def solution(mesh):
    in_specs = (
        P("ens", "space", None),
        P("space", None),
        P("space", None),
        P(),
        P("space"),
        P("space"),
        P("space"),
    )
    out_specs = (P("ens", "space", None), P("ens", "space", None))
    return jax.shard_map(shards, mesh=mesh, in_specs=in_specs, out_specs=out_specs, check_vma=False)
```

```python
import functools
import jax
import jax.numpy as jnp
from jax import lax
from jax.experimental import pallas as pl
from jax.experimental.pallas import tpu as pltpu
from jax.sharding import PartitionSpec as P

time_step = 0.11
steps = 32
halo = 8
sub = 8
lane = 128
pad = 8
MESH = pl.DeviceIdType.MESH


def dot(left, right, right_dim, left_dim=1):
    return lax.dot_general(
        left, right, (((left_dim,), (right_dim,)), ((), ())),
        precision=lax.Precision.HIGHEST, preferred_element_type=jnp.float32,
    )


def split_pieces(row):
    return [row[:, p * lane : (p + 1) * lane] for p in range(row.shape[1] // lane)]


def swap_piece_and_lane(pieces):
    count = len(pieces)
    lanes = lax.broadcasted_iota(jnp.int32, pieces[0].shape, 1)
    bit = 1
    while bit < count:
        upper = (lanes & bit) > 0
        out = list(pieces)
        for p in range(count):
            if p & bit:
                continue
            low, high = pieces[p], pieces[p + bit]
            out[p] = jnp.where(upper, pltpu.roll(high, bit, 1), low)
            out[p + bit] = jnp.where(upper, high, pltpu.roll(low, lane - bit, 1))
        pieces = out
        bit *= 2
    return pieces


def take_lanes(pieces, index):
    return [jnp.take_along_axis(p, index, axis=1, mode="promise_in_bounds") for p in pieces]


def to_strided(row):
    pieces = swap_piece_and_lane(split_pieces(row))
    count = len(pieces)
    lanes = lax.broadcasted_iota(jnp.int32, pieces[0].shape, 1)
    run = lane // count
    shift = run.bit_length() - 1
    return jnp.concatenate(take_lanes(pieces, (lanes & (run - 1)) * count + (lanes >> shift)), axis=1)


def to_natural(row):
    pieces = split_pieces(row)
    count = len(pieces)
    lanes = lax.broadcasted_iota(jnp.int32, pieces[0].shape, 1)
    shift = count.bit_length() - 1
    index = (lanes & (count - 1)) * (lane // count) + (lanes >> shift)
    return jnp.concatenate(swap_piece_and_lane(take_lanes(pieces, index)), axis=1)


def diffuse(h, slip):
    square = h * h
    return (slip * square) * pl.reciprocal(1.0 + square, approx=True)


def sweep(source, target, slip_ref, bal_ref, mask, first, count, turns):
    lanes = lax.broadcasted_iota(jnp.int32, (sub, lane), 1)
    at_end = lanes == lane - 1
    at_start = lanes == 0

    def load(row):
        h = source[pad + row]
        return h, diffuse(h, slip_ref[pad + row])

    def body(turn, carry):
        begin = first + turn * count
        h, d, f_up = carry
        for k in range(count):
            row = begin + k
            h_below, d_below = load(row + 1)
            f_down = (d_below + d) * (h_below - h)
            wrapped_h = jnp.where(at_end, 0.0, pltpu.roll(h[:, :lane], lane - 1, 1))
            wrapped_d = jnp.where(at_end, 0.0, pltpu.roll(d[:, :lane], lane - 1, 1))
            h_next = jnp.concatenate([h[:, lane:], wrapped_h], axis=1)
            d_next = jnp.concatenate([d[:, lane:], wrapped_d], axis=1)
            f_right = (d_next + d) * (h_next - h)
            edge = jnp.where(
                at_start, d[:, :lane] * h[:, :lane], pltpu.roll(f_right[:, -lane:], 1, 1)
            )
            f_left = jnp.concatenate([edge, f_right[:, :-lane]], axis=1)
            change = (f_down - f_up) + (f_right - f_left)
            balance = jnp.broadcast_to(bal_ref[pl.ds(pad + row, 1)], h.shape)
            moved = (h + balance) + change
            target[pad + row] = jnp.where(mask(row), moved, h)
            h, d, f_up = h_below, d_below, f_down
        return h, d, f_up

    h_above, d_above = load(first - 1)
    h, d = load(first)
    carry = (h, d, (d + d_above) * (h - h_above))
    if turns == 1:
        body(0, carry)
    else:
        lax.fori_loop(0, turns, body, carry)


def kernel(
    spaces, enss, params_ref, base_hbm, balance_hbm, count_hbm, index_hbm, observed_hbm, noise_hbm,
    out_ref, parts_ref, weights_ref, own_ref,
    count_ref, observed_ref, noise_ref, raw_ref, par_ref, bb_ref, index_land, even_ref, odd_ref, slip_ref, base_c, bal_c, land_ref, sent_ref,
    one_hot_ref, pick_ref, pred_ref, stage_ref, turned_ref, sum_ref, sum_land,
    raw_send, raw_recv, bb_send, bb_recv, index_send, index_recv, ens_send, ens_recv, local_sem,
    edge_send, edge_recv, h_send, h_recv, pred_send, pred_recv, thick_send, thick_recv,
    sum_send, sum_recv,
):
    rows, width = base_hbm.shape
    members = params_ref.shape[0]
    quad = members // sub
    groups = quad * enss
    total = quad * rows
    every = members * enss
    blocks = steps // halo
    count_obs = index_hbm.shape[1]
    pieces = width // lane

    me = lax.axis_index("space")
    ens = lax.axis_index("ens")
    pos = lax.rem(me, quad)
    home = me - pos
    has_up = home > 0
    has_down = home + quad < spaces
    up = jnp.maximum(me - quad, 0)
    down = jnp.minimum(me + quad, spaces - 1)
    sides = ((has_up, up, 1), (has_down, down, 0))

    twin = pos + 1 - 2 * lax.rem(pos, 2)
    far = [lax.rem(pos + 2, quad), lax.rem(twin + 2, quad)] if quad > 2 else []
    mates = far + [twin] * (quad > 1)
    others = [lax.rem(ens + d, enss) for d in range(1, enss)]
    peers = [
        (lax.rem(pos + d, quad), lax.rem(ens + e, enss))
        for d in range(quad) for e in range(enss) if d or e
    ]
    stages = spaces.bit_length() - 1
    inner = quad.bit_length() - 1
    bits = [0] + list(range(max(inner, 1), stages)) + list(range(1, inner))
    bits = bits[:stages]
    partners = []
    for stage in bits:
        bit = 1 << stage
        partners.append(me + bit - 2 * bit * lax.rem(lax.div(me, bit), 2))

    fetches = [
        pltpu.make_async_copy(source, dest, local_sem.at[k])
        for k, (source, dest) in enumerate((
            (params_ref.at[pl.ds(pos * sub, sub)], raw_ref.at[pos]),
            (base_hbm, bb_ref.at[0, pos]),
            (balance_hbm, bb_ref.at[1, pos]),
            (count_hbm, count_ref),
            (index_hbm, index_land.at[pos]),
            (observed_hbm, observed_ref),
            (noise_hbm, noise_ref),
            (params_ref, own_ref),
            (params_ref, par_ref.at[ens]),
        ))
    ]
    own_raw, own_params = fetches[0], fetches[-1]
    barrier = pltpu.get_barrier_semaphore()
    for mate, other in peers:
        pl.semaphore_signal(
            barrier, inc=1, device_id={"space": home + mate, "ens": other}, device_id_type=MESH
        )
    for have, target, _ in sides:
        @pl.when(have)
        def _(target=target):
            pl.semaphore_signal(barrier, inc=1, device_id={"space": target}, device_id_type=MESH)
    outer = [partner for bit, partner in zip(bits, partners) if bit >= inner]
    for partner in outer:
        pl.semaphore_signal(barrier, inc=1, device_id={"space": partner}, device_id_type=MESH)
    for fetch in fetches:
        fetch.start()
    pl.semaphore_wait(
        barrier, len(peers) + len(outer) + has_up.astype(jnp.int32) + has_down.astype(jnp.int32)
    )

    def raw_copy(mate, source, slot):
        return pltpu.make_async_remote_copy(
            params_ref.at[pl.ds(mate * sub, sub)], raw_ref.at[source],
            raw_send.at[slot], raw_recv.at[source],
            device_id={"space": home + mate}, device_id_type=MESH,
        )

    def bb_copy(which, mate, source, slot, passed=False):
        ref = bb_ref.at[which, source] if passed else (base_hbm, balance_hbm)[which]
        return pltpu.make_async_remote_copy(
            ref, bb_ref.at[which, source], bb_send.at[which, slot], bb_recv.at[which, source],
            device_id={"space": home + mate}, device_id_type=MESH,
        )

    def index_copy(mate, source, slot):
        return pltpu.make_async_remote_copy(
            index_hbm, index_land.at[source], index_send.at[slot], index_recv.at[source],
            device_id={"space": home + mate}, device_id_type=MESH,
        )

    def ens_copy(step, source):
        return pltpu.make_async_remote_copy(
            params_ref, par_ref.at[source], ens_send.at[step], ens_recv.at[source],
            device_id={"ens": others[step]}, device_id_type=MESH,
        )

    for slot, mate in enumerate(mates):
        if slot != 1:
            for which in range(2):
                bb_copy(which, mate, pos, slot).start()
        raw_copy(mate, pos, slot).start()
    for slot, mate in enumerate(mates):
        index_copy(mate, pos, slot).start()
    for step in range(enss - 1):
        ens_copy(step, ens).start()

    for fetch in fetches[1:-2]:
        fetch.wait()
    counts = count_ref[...].astype(jnp.float32)
    first_member = ens * members + pos * sub
    mine = (
        lax.broadcasted_iota(jnp.int32, (sub, every), 1)
        == lax.broadcasted_iota(jnp.int32, (sub, every), 0) + first_member
    )
    count = jnp.broadcast_to(
        jnp.sum(jnp.where(mine, jnp.broadcast_to(counts, (sub, every)), 0.0), axis=1, keepdims=True),
        (sub, lane),
    )

    zero = jnp.zeros((sub, width), jnp.float32)
    for side, (have, _, _) in enumerate(sides):
        begin = pad - halo if side == 0 else pad + total

        @pl.when(jnp.logical_not(have))
        def _(side=side, begin=begin):
            for row in range(halo):
                slip_ref[begin + row] = zero
                even_ref[begin + row] = zero
                odd_ref[begin + row] = zero
            edge = 0 if side == 0 else pad + total
            base_c[pl.ds(edge, pad)] = zero
            bal_c[pl.ds(edge, pad)] = zero

    def use_bb(source):
        @pl.loop(0, rows // sub)
        def _(tile):
            at = pl.multiple_of(tile * sub, sub)
            to = pl.multiple_of(pad + source * rows + at, sub)
            base_c[pl.ds(to, sub)] = to_strided(bb_ref[0, source, pl.ds(at, sub)])
            bal_c[pl.ds(to, sub)] = to_strided(bb_ref[1, source, pl.ds(at, sub)] * time_step)

        @pl.loop(0, rows)
        def _(row):
            at = source * rows + row + pad
            even_ref[at] = jnp.broadcast_to(base_c[pl.ds(at, 1)], (sub, width))

    def use_raw(source):
        @pl.loop(0, rows // sub)
        def _(tile):
            at = pl.multiple_of(tile * sub, sub)
            turned = jnp.swapaxes(raw_ref[source, :, pl.ds(at, sub)], 0, 1)
            slip = (jnp.exp(turned) * (0.5 * time_step)).reshape(sub * sub, width)
            slip_ref[pl.ds(pad + source * rows + at, sub)] = to_strided(slip).reshape(sub, sub, width)

    use_bb(pos)
    own_raw.wait()
    use_raw(pos)
    for slot, mate in enumerate(mates):
        for which in range(2):
            bb_copy(which, mate, mate, 0).wait_recv()
            if far and slot == 0:
                bb_copy(which, twin, mate, 1, True).start()
    for mate in mates:
        use_bb(mate)
    for mate in mates:
        index_copy(mate, mate, 0).wait_recv()

    shift = width.bit_length() - 1
    turn = pieces.bit_length() - 1

    def place_of(source):
        index = index_land[source]
        column = index & (width - 1)
        return index >> shift, (column & (pieces - 1)) * lane + (column >> turn)

    @pl.loop(0, quad)
    def _(source):
        _, place = place_of(source)
        one_hot_ref[source] = jnp.where(
            lax.broadcasted_iota(jnp.int32, (width, count_obs), 0) == place, 1.0, 0.0
        ).astype(jnp.bfloat16)

    for mate in reversed(mates):
        raw_copy(mate, mate, 0).wait_recv()
        use_raw(mate)

    def edge_copies(side):
        _, target, there = sides[side]
        slip_from = pad if side == 0 else pad + total - halo
        slip_to = pad + total if side == 0 else pad - halo
        row_from = pad if side == 0 else total
        row_to = pad + total if side == 0 else 0
        pairs = (
            (slip_ref.at[pl.ds(slip_from, halo)], slip_ref.at[pl.ds(slip_to, halo)]),
            (base_c.at[pl.ds(row_from, pad)], base_c.at[pl.ds(row_to, pad)]),
            (bal_c.at[pl.ds(row_from, pad)], bal_c.at[pl.ds(row_to, pad)]),
        )
        return [
            pltpu.make_async_remote_copy(
                source, dest, edge_send.at[side, k], edge_recv.at[there, k],
                device_id={"space": target}, device_id_type=MESH,
            )
            for k, (source, dest) in enumerate(pairs)
        ]

    def edge_arrivals(side):
        _, target, _ = sides[side]
        slip_at = pad - halo if side == 0 else pad + total
        row_at = 0 if side == 0 else pad + total
        refs = (
            slip_ref.at[pl.ds(slip_at, halo)], base_c.at[pl.ds(row_at, pad)],
            bal_c.at[pl.ds(row_at, pad)],
        )
        return [
            pltpu.make_async_remote_copy(
                ref, ref, edge_send.at[side, k], edge_recv.at[side, k],
                device_id={"space": target}, device_id_type=MESH,
            )
            for k, ref in enumerate(refs)
        ]

    for side in range(2):
        @pl.when(sides[side][0])
        def _(side=side):
            for copy in edge_copies(side):
                copy.start()

    def h_copy(side, slot):
        _, target, there = sides[side]
        return pltpu.make_async_remote_copy(
            sent_ref.at[slot, side], land_ref.at[slot, there],
            h_send.at[slot, side], h_recv.at[slot, there],
            device_id={"space": target}, device_id_type=MESH,
        )

    def h_arrival(side, slot):
        _, target, _ = sides[side]
        return pltpu.make_async_remote_copy(
            sent_ref.at[slot, side], land_ref.at[slot, side],
            h_send.at[slot, side], h_recv.at[slot, side],
            device_id={"space": target}, device_id_type=MESH,
        )

    beyond = (count * has_up.astype(jnp.float32), count * has_down.astype(jnp.float32))

    @pl.loop(0, blocks)
    def _(block):
        slot = lax.rem(block, 2)
        begin = (block * halo).astype(jnp.float32)
        buffers = (even_ref, odd_ref)

        def wide(mask):
            return jnp.concatenate([mask] * pieces, axis=1)

        for level in range(1, halo + 1):
            active = wide((begin + float(level - 1)) < count)
            sweep(
                buffers[(level - 1) % 2], buffers[level % 2], slip_ref, bal_c,
                lambda row: active, level, total // 2 - level, 2,
            )

        for side in range(2):
            at = pad - halo if side == 0 else pad + total

            @pl.when(jnp.logical_and(sides[side][0], block == 0))
            def _(side=side, at=at):
                for copy in edge_arrivals(side):
                    copy.wait_recv()
                for row in range(halo):
                    even_ref[at + row] = jnp.broadcast_to(base_c[pl.ds(at + row, 1)], (sub, width))

            @pl.when(jnp.logical_and(sides[side][0], block > 0))
            def _(side=side, at=at):
                h_arrival(side, slot).wait_recv()
                even_ref[pl.ds(at, halo)] = land_ref[slot, side]

            @pl.when(jnp.logical_and(sides[side][0], block > 1))
            def _(side=side):
                h_copy(side, 1 - slot).wait_send()

        @pl.loop(0, halo // 2)
        def _(pair):
            for odd in range(2):
                level = pair * 2 + (odd + 1)
                now = begin + (level - 1).astype(jnp.float32)
                for side in range(2):
                    first = level - halo if side == 0 else total - level

                    def mask(row, side=side, now=now):
                        outside = row < 0 if side == 0 else row >= total
                        return wide(now < jnp.where(outside, beyond[side], count))

                    sweep(
                        buffers[odd], buffers[1 - odd], slip_ref, bal_c, mask, first, halo, 1
                    )

        for side in range(2):
            at = pad if side == 0 else pad + total - halo
            sent_ref[1 - slot, side] = even_ref[pl.ds(at, halo)]

        for side in range(2):
            @pl.when(jnp.logical_and(sides[side][0], block < blocks - 1))
            def _(side=side):
                h_copy(side, 1 - slot).start()

    for source in range(quad):
        cells = even_ref[pl.ds(pad + source * rows, rows)].reshape(rows * sub, width)
        picked = None
        one_hot = one_hot_ref[source]
        for part in range(3):
            cut = cells.astype(jnp.bfloat16)
            if part < 2:
                cells = cells - cut.astype(jnp.float32)
            term = jnp.dot(cut, one_hot, preferred_element_type=jnp.float32)
            picked = term if picked is None else picked + term
        row_at, _ = place_of(source)
        at_row = lax.broadcasted_iota(jnp.int32, (rows, sub, count_obs), 0) == row_at
        pick_ref[source] = jnp.sum(
            jnp.where(at_row, picked.reshape(rows, sub, count_obs), 0.0), axis=0
        )

    def pred_copy(k, source_ens, source_pos):
        mate, other = peers[k]
        return pltpu.make_async_remote_copy(
            pick_ref.at[mate], pred_ref.at[source_ens, source_pos],
            pred_send.at[k], pred_recv.at[source_ens, source_pos],
            device_id={"space": home + mate, "ens": other}, device_id_type=MESH,
        )

    for k in range(len(peers)):
        pred_copy(k, ens, pos).start()
    pred_ref[ens, pos] = pick_ref[pos]

    def thick_copy(mate, source, slot):
        return pltpu.make_async_remote_copy(
            stage_ref.at[mate], out_ref.at[pl.ds(source * sub, sub)],
            thick_send.at[slot], thick_recv.at[source],
            device_id={"space": home + mate}, device_id_type=MESH,
        )

    def unturn(mate):
        @pl.loop(0, rows // sub)
        def _(tile):
            at = pl.multiple_of(tile * sub, sub)
            cells = even_ref[pl.ds(pad + mate * rows + at, sub)].reshape(sub * sub, width)
            stage_ref[mate, :, pl.ds(at, sub)] = jnp.swapaxes(
                to_natural(cells).reshape(sub, sub, width), 0, 1
            )

    for slot, mate in enumerate(mates):
        unturn(mate)
        thick_copy(mate, pos, slot).start()
    unturn(pos)
    own_thick = pltpu.make_async_copy(
        stage_ref.at[pos], out_ref.at[pl.ds(pos * sub, sub)], local_sem.at[9]
    )
    own_thick.start()
    for k, (mate, other) in enumerate(peers):
        pred_copy(k, other, mate).wait_recv()

    scaling = lax.rsqrt(noise_ref[...])
    predicted = pred_ref[...].reshape(every, count_obs)
    average = jnp.sum(predicted, axis=0, keepdims=True) * (1.0 / every)
    root = jnp.sqrt(jnp.float32(every - 1))
    anomalies = (predicted - average) * (scaling / root)
    surprise = (observed_ref[...] - average) * scaling
    spread = sum_ref.shape[2]
    first = lax.broadcasted_iota(jnp.int32, (spread - every, count_obs), 0) == 0
    lower = jnp.where(first, jnp.broadcast_to(surprise, first.shape), 0.0)
    sum_ref[0] = dot(anomalies, jnp.concatenate([anomalies, lower], axis=0), 1)

    def sum_copy(stage):
        return pltpu.make_async_remote_copy(
            sum_ref.at[stage], sum_land.at[stage], sum_send.at[stage], sum_recv.at[stage],
            device_id={"space": partners[stage]}, device_id_type=MESH,
        )

    for stage in range(stages):
        sum_copy(stage).start()
        if stage == min(1, stages - 1):
            fetches[-2].wait()
            own_params.wait()
            for step in range(enss - 1):
                ens_copy(step, others[step]).wait_recv()

            @pl.loop(0, groups)
            def _(group):
                member = pl.multiple_of(lax.rem(group, quad) * sub, sub)
                turned_ref[group] = jnp.swapaxes(
                    par_ref[lax.div(group, quad), pl.ds(member, sub)], 0, 1
                )

            @pl.loop(0, rows)
            def _(row):
                values = turned_ref[:, row].reshape(every, width)
                middle = jnp.sum(turned_ref[:, row], axis=0)
                middle = jnp.sum(middle, axis=0, keepdims=True) * (1.0 / every)
                deviation = values - middle
                high = deviation.astype(jnp.bfloat16)
                parts_ref[row, pl.ds(0, every)] = high
                parts_ref[row, pl.ds(every, every)] = (
                    deviation - high.astype(jnp.float32)
                ).astype(jnp.bfloat16)

        sum_copy(stage).wait_recv()
        sum_ref[stage + 1] = sum_ref[stage] + sum_land[stage]

    row_of = lax.broadcasted_iota(jnp.int32, (every, spread), 0)
    lane_of = lax.broadcasted_iota(jnp.int32, (every, spread), 1)
    own_unit = (row_of + (every + 1) == lane_of + ens * members) & (lane_of > every)
    unit = (row_of == lane_of) | own_unit
    system = sum_ref[stages] + jnp.where(unit, 1.0, 0.0)
    for pivot in range(0, every, 4):
        four = range(4)
        columns = [
            jnp.broadcast_to(system[:, pivot + k : pivot + k + 1], (every, spread)) for k in four
        ]
        lines = [system[pivot + k : pivot + k + 1] for k in four]
        m = [[columns[j][pivot + i : pivot + i + 1] for j in four] for i in four]
        scale = 1.0 / (m[0][0] * m[1][1] - m[0][1] * m[1][0])

        def first_pair(x, y, m=m, scale=scale):
            return (m[1][1] * x - m[0][1] * y) * scale, (m[0][0] * y - m[1][0] * x) * scale

        b = [first_pair(m[0][k], m[1][k]) for k in (2, 3)]
        new = list(first_pair(lines[0], lines[1]))
        d = [[m[i][2 + k] - m[i][0] * b[k][0] - m[i][1] * b[k][1] for k in (0, 1)] for i in (2, 3)]
        y = [lines[i] - m[i][0] * new[0] - m[i][1] * new[1] for i in (2, 3)]
        scale = 1.0 / (d[0][0] * d[1][1] - d[0][1] * d[1][0])
        new.append((d[1][1] * y[0] - d[0][1] * y[1]) * scale)
        new.append((d[0][0] * y[1] - d[1][0] * y[0]) * scale)
        for i in (0, 1):
            new[i] = new[i] - b[0][i] * new[2] - b[1][i] * new[3]
        rest = system
        for k in four:
            rest = rest - columns[k] * new[k]
        for k in four:
            rest = jnp.where(row_of == pivot + k, new[k], rest)
        system = rest
    gain = system[:, every : every + 1] / root
    weights = system[:, every + 1 : every + 1 + members] + gain
    weights = weights - jnp.where(
        lax.broadcasted_iota(jnp.int32, (every, members), 0)
        == lax.broadcasted_iota(jnp.int32, (every, members), 1) + ens * members, 1.0, 0.0,
    )
    weights = weights.T
    high = weights.astype(jnp.bfloat16)
    low = (weights - high.astype(jnp.float32)).astype(jnp.bfloat16)
    weights_ref[...] = jnp.concatenate([
        jnp.concatenate([high, high], axis=1), jnp.concatenate([low, low], axis=1)
    ], axis=0)

    for mate in mates:
        thick_copy(mate, mate, 0).wait_recv()
    own_thick.wait()
    for slot, mate in enumerate(mates):
        for which in range(2):
            if slot == 1:
                bb_copy(which, twin, far[0], slot, True).wait_send()
            else:
                bb_copy(which, mate, pos, slot).wait_send()
        raw_copy(mate, pos, slot).wait_send()
        index_copy(mate, pos, slot).wait_send()
        thick_copy(mate, pos, slot).wait_send()
    for step in range(enss - 1):
        ens_copy(step, ens).wait_send()
    for k in range(len(peers)):
        pred_copy(k, ens, pos).wait_send()
    for stage in range(stages):
        sum_copy(stage).wait_send()
    for side in range(2):
        @pl.when(sides[side][0])
        def _(side=side):
            for copy in edge_copies(side):
                copy.wait_send()
            h_copy(side, (blocks - 1) % 2).wait_send()


def finish_kernel(thick_ref, params_ref, parts_ref, weights_ref, out_ref, updated_ref, made_ref, sem):
    members, rows, width = params_ref.shape
    quad = members // sub
    thick = pltpu.make_async_copy(thick_ref, out_ref, sem.at[0])
    thick.start()
    weights = weights_ref[...]
    copies = []
    for tile in range(rows // sub):
        here = pl.ds(tile * sub, sub)
        steps_made = []
        for k in range(sub):
            both = jnp.dot(
                weights, parts_ref[tile * sub + k], preferred_element_type=jnp.float32
            )
            steps_made.append(both[:members] + both[members:])
        for group in range(quad):
            own = slice(group * sub, (group + 1) * sub)
            made = jnp.stack([step[own] for step in steps_made])
            there = pl.ds(group * sub, sub)
            made_ref[there, here] = params_ref[there, here] + jnp.swapaxes(made, 0, 1)
            copies.append(pltpu.make_async_copy(
                made_ref.at[there, here], updated_ref.at[there, here], sem.at[1 + len(copies)]
            ))
            copies[-1].start()
    for copy in copies:
        copy.wait()
    thick.wait()


def shards(params, base_thickness, balance, step_count, obs_index, observed, noise_var):
    members, rows, width = params.shape
    spaces, enss = lax.axis_size("space"), lax.axis_size("ens")
    quad = members // sub
    total = quad * rows
    every = members * enss
    count_obs = obs_index.shape[0]
    spread = pl.cdiv(every + 1 + members, lane) * lane
    stages = spaces.bit_length() - 1
    assert 1 << stages == spaces and spaces % quad == 0 and quad in (1, 2, 4)
    assert width & (width - 1) == 0 and steps // halo > 2
    dma = pltpu.SemaphoreType.DMA
    vmem = pl.BlockSpec(memory_space=pltpu.VMEM)
    f32 = jnp.float32
    many = max(quad - 1, 1)
    flat = jax.ShapeDtypeStruct(params.shape, f32)
    thick, parts, weights, own = pl.pallas_call(
        functools.partial(kernel, spaces, enss),
        out_shape=(
            flat,
            jax.ShapeDtypeStruct((rows, 2 * every, width), jnp.bfloat16),
            jax.ShapeDtypeStruct((2 * members, 2 * every), jnp.bfloat16),
            flat,
        ),
        in_specs=[pl.BlockSpec(memory_space=pltpu.HBM)] * 7,
        out_specs=(vmem,) * 4,
        scratch_shapes=[
            pltpu.VMEM((1, every), jnp.int32),
            pltpu.VMEM((1, count_obs), f32),
            pltpu.VMEM((1, count_obs), f32),
            pltpu.VMEM((quad, sub, rows, width), f32),
            pltpu.VMEM((enss, members, rows, width), f32),
            pltpu.VMEM((2, quad, rows, width), f32),
            pltpu.VMEM((quad, 1, count_obs), jnp.int32),
            pltpu.VMEM((total + 2 * pad, sub, width), f32),
            pltpu.VMEM((total + 2 * pad, sub, width), f32),
            pltpu.VMEM((total + 2 * pad, sub, width), f32),
            pltpu.VMEM((total + 2 * pad, width), f32),
            pltpu.VMEM((total + 2 * pad, width), f32),
            pltpu.VMEM((2, 2, halo, sub, width), f32),
            pltpu.VMEM((2, 2, halo, sub, width), f32),
            pltpu.VMEM((quad, width, count_obs), jnp.bfloat16),
            pltpu.VMEM((quad, sub, count_obs), f32),
            pltpu.VMEM((enss, quad, sub, count_obs), f32),
            pltpu.VMEM((quad, sub, rows, width), f32),
            pltpu.VMEM((quad * enss, rows, sub, width), f32),
            pltpu.VMEM((stages + 1, every, spread), f32),
            pltpu.VMEM((stages, every, spread), f32),
            dma((many,)), dma((quad,)),
            dma((2, many)), dma((2, quad)),
            dma((many,)), dma((quad,)),
            dma((max(enss - 1, 1),)), dma((enss,)),
            dma((10,)),
            dma((2, 3)), dma((2, 3)),
            dma((2, 2)), dma((2, 2)),
            dma((quad * enss,)), dma((enss, quad)),
            dma((many,)), dma((quad,)),
            dma((stages,)), dma((stages,)),
        ],
        compiler_params=pltpu.CompilerParams(
            collective_id=0, has_side_effects=True, vmem_limit_bytes=48 * 1024 * 1024
        ),
        name="advance",
    )(
        *(pltpu.with_memory_space_constraint(x, pltpu.HBM) for x in (
            params, base_thickness, balance, step_count[None],
            obs_index[None], observed[None], noise_var[None],
        ))
    )
    return pl.pallas_call(
        finish_kernel,
        out_shape=(flat, flat),
        in_specs=[vmem] * 4,
        out_specs=(pl.BlockSpec(memory_space=pltpu.HBM),) * 2,
        scratch_shapes=[pltpu.VMEM(params.shape, f32), dma((1 + quad * (rows // sub),))],
        compiler_params=pltpu.CompilerParams(vmem_limit_bytes=8 * 1024 * 1024),
        name="finish",
    )(thick, own, parts, weights)


def solution(mesh):
    in_specs = (
        P("ens", "space", None),
        P("space", None),
        P("space", None),
        P(),
        P("space"),
        P("space"),
        P("space"),
    )
    out_specs = (P("ens", "space", None), P("ens", "space", None))
    return jax.shard_map(shards, mesh=mesh, in_specs=in_specs, out_specs=out_specs, check_vma=False)
```

```python
import functools
import jax
import jax.numpy as jnp
from jax import lax
from jax.experimental import pallas as pl
from jax.experimental.pallas import tpu as pltpu
from jax.sharding import PartitionSpec as P

time_step = 0.11
steps = 32
halo = 8
sub = 8
lane = 128
pad = 8
MESH = pl.DeviceIdType.MESH


def dot(left, right, right_dim, left_dim=1):
    return lax.dot_general(
        left, right, (((left_dim,), (right_dim,)), ((), ())),
        precision=lax.Precision.HIGHEST, preferred_element_type=jnp.float32,
    )


def split_pieces(row):
    return [row[:, p * lane : (p + 1) * lane] for p in range(row.shape[1] // lane)]


def swap_piece_and_lane(pieces):
    count = len(pieces)
    lanes = lax.broadcasted_iota(jnp.int32, pieces[0].shape, 1)
    bit = 1
    while bit < count:
        upper = (lanes & bit) > 0
        out = list(pieces)
        for p in range(count):
            if p & bit:
                continue
            low, high = pieces[p], pieces[p + bit]
            out[p] = jnp.where(upper, pltpu.roll(high, bit, 1), low)
            out[p + bit] = jnp.where(upper, high, pltpu.roll(low, lane - bit, 1))
        pieces = out
        bit *= 2
    return pieces


def take_lanes(pieces, index):
    return [jnp.take_along_axis(p, index, axis=1, mode="promise_in_bounds") for p in pieces]


def to_strided(row):
    pieces = swap_piece_and_lane(split_pieces(row))
    count = len(pieces)
    lanes = lax.broadcasted_iota(jnp.int32, pieces[0].shape, 1)
    run = lane // count
    shift = run.bit_length() - 1
    return jnp.concatenate(take_lanes(pieces, (lanes & (run - 1)) * count + (lanes >> shift)), axis=1)


def to_natural(row):
    pieces = split_pieces(row)
    count = len(pieces)
    lanes = lax.broadcasted_iota(jnp.int32, pieces[0].shape, 1)
    shift = count.bit_length() - 1
    index = (lanes & (count - 1)) * (lane // count) + (lanes >> shift)
    return jnp.concatenate(swap_piece_and_lane(take_lanes(pieces, index)), axis=1)


def diffuse(h, slip):
    square = h * h
    return (slip * square) * pl.reciprocal(1.0 + square, approx=True)


def sweep(source, target, slip_ref, bal_ref, mask, first, count, turns):
    lanes = lax.broadcasted_iota(jnp.int32, (sub, lane), 1)
    at_end = lanes == lane - 1
    at_start = lanes == 0

    def load(row):
        h = source[pad + row]
        return h, diffuse(h, slip_ref[pad + row])

    def body(turn, carry):
        begin = first + turn * count
        h, d, f_up = carry
        for k in range(count):
            row = begin + k
            h_below, d_below = load(row + 1)
            f_down = (d_below + d) * (h_below - h)
            wrapped_h = jnp.where(at_end, 0.0, pltpu.roll(h[:, :lane], lane - 1, 1))
            wrapped_d = jnp.where(at_end, 0.0, pltpu.roll(d[:, :lane], lane - 1, 1))
            h_next = jnp.concatenate([h[:, lane:], wrapped_h], axis=1)
            d_next = jnp.concatenate([d[:, lane:], wrapped_d], axis=1)
            f_right = (d_next + d) * (h_next - h)
            edge = jnp.where(
                at_start, d[:, :lane] * h[:, :lane], pltpu.roll(f_right[:, -lane:], 1, 1)
            )
            f_left = jnp.concatenate([edge, f_right[:, :-lane]], axis=1)
            change = (f_down - f_up) + (f_right - f_left)
            balance = jnp.broadcast_to(bal_ref[pl.ds(pad + row, 1)], h.shape)
            moved = (h + balance) + change
            target[pad + row] = jnp.where(mask(row), moved, h)
            h, d, f_up = h_below, d_below, f_down
        return h, d, f_up

    h_above, d_above = load(first - 1)
    h, d = load(first)
    carry = (h, d, (d + d_above) * (h - h_above))
    if turns == 1:
        body(0, carry)
    else:
        lax.fori_loop(0, turns, body, carry)


def kernel(
    spaces, enss, params_ref, base_hbm, balance_hbm, count_hbm, index_hbm, observed_hbm, noise_hbm,
    out_ref, parts_ref, weights_ref, own_ref,
    count_ref, observed_ref, noise_ref, raw_ref, par_ref, bb_ref, index_land, even_ref, odd_ref, slip_ref, base_c, bal_c, land_ref, sent_ref,
    one_hot_ref, pick_ref, pred_ref, stage_ref, turned_ref, sum_ref, sum_land,
    raw_send, raw_recv, bb_send, bb_recv, index_send, index_recv, ens_send, ens_recv, local_sem,
    edge_send, edge_recv, h_send, h_recv, pred_send, pred_recv, thick_send, thick_recv,
    sum_send, sum_recv,
):
    rows, width = base_hbm.shape
    members = params_ref.shape[0]
    quad = members // sub
    groups = quad * enss
    total = quad * rows
    every = members * enss
    blocks = steps // halo
    count_obs = index_hbm.shape[1]
    pieces = width // lane

    me = lax.axis_index("space")
    ens = lax.axis_index("ens")
    pos = lax.rem(me, quad)
    home = me - pos
    has_up = home > 0
    has_down = home + quad < spaces
    up = jnp.maximum(me - quad, 0)
    down = jnp.minimum(me + quad, spaces - 1)
    sides = ((has_up, up, 1), (has_down, down, 0))

    twin = pos + 1 - 2 * lax.rem(pos, 2)
    far = [lax.rem(pos + 2, quad), lax.rem(twin + 2, quad)] if quad > 2 else []
    mates = far + [twin] * (quad > 1)
    others = [lax.rem(ens + d, enss) for d in range(1, enss)]
    peers = [
        (lax.rem(pos + d, quad), lax.rem(ens + e, enss))
        for d in range(quad) for e in range(enss) if d or e
    ]
    stages = spaces.bit_length() - 1
    inner = quad.bit_length() - 1
    outer = list(range(max(inner, 1), stages))
    bits = [[0]] + [outer[k : k + 2] for k in range(0, len(outer), 2)] + [[k] for k in range(1, inner)]

    def across(some):
        found = [me]
        for k in some:
            bit = 1 << k
            found += [at + bit - 2 * bit * lax.rem(lax.div(at, bit), 2) for at in found]
        return found[1:]

    partners = [across(some) for some in bits]

    fetches = [
        pltpu.make_async_copy(source, dest, local_sem.at[k])
        for k, (source, dest) in enumerate((
            (params_ref.at[pl.ds(pos * sub, sub)], raw_ref.at[pos]),
            (base_hbm, bb_ref.at[0, pos]),
            (balance_hbm, bb_ref.at[1, pos]),
            (count_hbm, count_ref),
            (index_hbm, index_land.at[pos]),
            (observed_hbm, observed_ref),
            (noise_hbm, noise_ref),
            (params_ref, own_ref),
            (params_ref, par_ref.at[ens]),
        ))
    ]
    own_raw, own_params = fetches[0], fetches[-1]
    barrier = pltpu.get_barrier_semaphore()
    for mate, other in peers:
        pl.semaphore_signal(
            barrier, inc=1, device_id={"space": home + mate, "ens": other}, device_id_type=MESH
        )
    for have, target, _ in sides:
        @pl.when(have)
        def _(target=target):
            pl.semaphore_signal(barrier, inc=1, device_id={"space": target}, device_id_type=MESH)
    beyond_quad = [at for some, found in zip(bits, partners) if some[0] >= inner for at in found]
    for partner in beyond_quad:
        pl.semaphore_signal(barrier, inc=1, device_id={"space": partner}, device_id_type=MESH)
    for fetch in fetches:
        fetch.start()
    pl.semaphore_wait(
        barrier, len(peers) + len(beyond_quad) + has_up.astype(jnp.int32) + has_down.astype(jnp.int32)
    )

    def raw_copy(mate, source, slot):
        return pltpu.make_async_remote_copy(
            params_ref.at[pl.ds(mate * sub, sub)], raw_ref.at[source],
            raw_send.at[slot], raw_recv.at[source],
            device_id={"space": home + mate}, device_id_type=MESH,
        )

    def bb_copy(which, mate, source, slot, passed=False):
        ref = bb_ref.at[which, source] if passed else (base_hbm, balance_hbm)[which]
        return pltpu.make_async_remote_copy(
            ref, bb_ref.at[which, source], bb_send.at[which, slot], bb_recv.at[which, source],
            device_id={"space": home + mate}, device_id_type=MESH,
        )

    def index_copy(mate, source, slot):
        return pltpu.make_async_remote_copy(
            index_hbm, index_land.at[source], index_send.at[slot], index_recv.at[source],
            device_id={"space": home + mate}, device_id_type=MESH,
        )

    def ens_copy(step, source):
        return pltpu.make_async_remote_copy(
            params_ref, par_ref.at[source], ens_send.at[step], ens_recv.at[source],
            device_id={"ens": others[step]}, device_id_type=MESH,
        )

    for slot, mate in enumerate(mates):
        if slot != 1:
            for which in range(2):
                bb_copy(which, mate, pos, slot).start()
        raw_copy(mate, pos, slot).start()
    for slot, mate in enumerate(mates):
        index_copy(mate, pos, slot).start()
    for step in range(enss - 1):
        ens_copy(step, ens).start()

    for fetch in fetches[1:-2]:
        fetch.wait()
    counts = count_ref[...].astype(jnp.float32)
    first_member = ens * members + pos * sub
    mine = (
        lax.broadcasted_iota(jnp.int32, (sub, every), 1)
        == lax.broadcasted_iota(jnp.int32, (sub, every), 0) + first_member
    )
    count = jnp.broadcast_to(
        jnp.sum(jnp.where(mine, jnp.broadcast_to(counts, (sub, every)), 0.0), axis=1, keepdims=True),
        (sub, lane),
    )

    zero = jnp.zeros((sub, width), jnp.float32)
    for side, (have, _, _) in enumerate(sides):
        begin = pad - halo if side == 0 else pad + total

        @pl.when(jnp.logical_not(have))
        def _(side=side, begin=begin):
            for row in range(halo):
                slip_ref[begin + row] = zero
                even_ref[begin + row] = zero
                odd_ref[begin + row] = zero
            edge = 0 if side == 0 else pad + total
            base_c[pl.ds(edge, pad)] = zero
            bal_c[pl.ds(edge, pad)] = zero

    def use_bb(source):
        @pl.loop(0, rows // sub)
        def _(tile):
            at = pl.multiple_of(tile * sub, sub)
            to = pl.multiple_of(pad + source * rows + at, sub)
            base_c[pl.ds(to, sub)] = to_strided(bb_ref[0, source, pl.ds(at, sub)])
            bal_c[pl.ds(to, sub)] = to_strided(bb_ref[1, source, pl.ds(at, sub)] * time_step)

        @pl.loop(0, rows)
        def _(row):
            at = source * rows + row + pad
            even_ref[at] = jnp.broadcast_to(base_c[pl.ds(at, 1)], (sub, width))

    def use_raw(source):
        @pl.loop(0, rows // sub)
        def _(tile):
            at = pl.multiple_of(tile * sub, sub)
            turned = jnp.swapaxes(raw_ref[source, :, pl.ds(at, sub)], 0, 1)
            slip = (jnp.exp(turned) * (0.5 * time_step)).reshape(sub * sub, width)
            slip_ref[pl.ds(pad + source * rows + at, sub)] = to_strided(slip).reshape(sub, sub, width)

    use_bb(pos)
    own_raw.wait()
    use_raw(pos)
    for slot, mate in enumerate(mates):
        for which in range(2):
            bb_copy(which, mate, mate, 0).wait_recv()
            if far and slot == 0:
                bb_copy(which, twin, mate, 1, True).start()
    for mate in mates:
        use_bb(mate)
    for mate in mates:
        index_copy(mate, mate, 0).wait_recv()

    shift = width.bit_length() - 1
    turn = pieces.bit_length() - 1

    def place_of(source):
        index = index_land[source]
        column = index & (width - 1)
        return index >> shift, (column & (pieces - 1)) * lane + (column >> turn)

    @pl.loop(0, quad)
    def _(source):
        _, place = place_of(source)
        one_hot_ref[source] = jnp.where(
            lax.broadcasted_iota(jnp.int32, (width, count_obs), 0) == place, 1.0, 0.0
        ).astype(jnp.bfloat16)

    for mate in reversed(mates):
        raw_copy(mate, mate, 0).wait_recv()
        use_raw(mate)

    def edge_copies(side):
        _, target, there = sides[side]
        slip_from = pad if side == 0 else pad + total - halo
        slip_to = pad + total if side == 0 else pad - halo
        row_from = pad if side == 0 else total
        row_to = pad + total if side == 0 else 0
        pairs = (
            (slip_ref.at[pl.ds(slip_from, halo)], slip_ref.at[pl.ds(slip_to, halo)]),
            (base_c.at[pl.ds(row_from, pad)], base_c.at[pl.ds(row_to, pad)]),
            (bal_c.at[pl.ds(row_from, pad)], bal_c.at[pl.ds(row_to, pad)]),
        )
        return [
            pltpu.make_async_remote_copy(
                source, dest, edge_send.at[side, k], edge_recv.at[there, k],
                device_id={"space": target}, device_id_type=MESH,
            )
            for k, (source, dest) in enumerate(pairs)
        ]

    def edge_arrivals(side):
        _, target, _ = sides[side]
        slip_at = pad - halo if side == 0 else pad + total
        row_at = 0 if side == 0 else pad + total
        refs = (
            slip_ref.at[pl.ds(slip_at, halo)], base_c.at[pl.ds(row_at, pad)],
            bal_c.at[pl.ds(row_at, pad)],
        )
        return [
            pltpu.make_async_remote_copy(
                ref, ref, edge_send.at[side, k], edge_recv.at[side, k],
                device_id={"space": target}, device_id_type=MESH,
            )
            for k, ref in enumerate(refs)
        ]

    for side in range(2):
        @pl.when(sides[side][0])
        def _(side=side):
            for copy in edge_copies(side):
                copy.start()

    def h_copy(side, slot):
        _, target, there = sides[side]
        return pltpu.make_async_remote_copy(
            sent_ref.at[slot, side], land_ref.at[slot, there],
            h_send.at[slot, side], h_recv.at[slot, there],
            device_id={"space": target}, device_id_type=MESH,
        )

    def h_arrival(side, slot):
        _, target, _ = sides[side]
        return pltpu.make_async_remote_copy(
            sent_ref.at[slot, side], land_ref.at[slot, side],
            h_send.at[slot, side], h_recv.at[slot, side],
            device_id={"space": target}, device_id_type=MESH,
        )

    beyond = (count * has_up.astype(jnp.float32), count * has_down.astype(jnp.float32))

    @pl.loop(0, blocks)
    def _(block):
        slot = lax.rem(block, 2)
        begin = (block * halo).astype(jnp.float32)
        buffers = (even_ref, odd_ref)

        def wide(mask):
            return jnp.concatenate([mask] * pieces, axis=1)

        for level in range(1, halo + 1):
            active = wide((begin + float(level - 1)) < count)
            sweep(
                buffers[(level - 1) % 2], buffers[level % 2], slip_ref, bal_c,
                lambda row: active, level, total // 2 - level, 2,
            )

        for side in range(2):
            at = pad - halo if side == 0 else pad + total

            @pl.when(jnp.logical_and(sides[side][0], block == 0))
            def _(side=side, at=at):
                for copy in edge_arrivals(side):
                    copy.wait_recv()
                for row in range(halo):
                    even_ref[at + row] = jnp.broadcast_to(base_c[pl.ds(at + row, 1)], (sub, width))

            @pl.when(jnp.logical_and(sides[side][0], block > 0))
            def _(side=side, at=at):
                h_arrival(side, slot).wait_recv()
                even_ref[pl.ds(at, halo)] = land_ref[slot, side]

            @pl.when(jnp.logical_and(sides[side][0], block > 1))
            def _(side=side):
                h_copy(side, 1 - slot).wait_send()

        @pl.loop(0, halo // 2)
        def _(pair):
            for odd in range(2):
                level = pair * 2 + (odd + 1)
                now = begin + (level - 1).astype(jnp.float32)
                for side in range(2):
                    first = level - halo if side == 0 else total - level

                    def mask(row, side=side, now=now):
                        outside = row < 0 if side == 0 else row >= total
                        return wide(now < jnp.where(outside, beyond[side], count))

                    sweep(
                        buffers[odd], buffers[1 - odd], slip_ref, bal_c, mask, first, halo, 1
                    )

        for side in range(2):
            at = pad if side == 0 else pad + total - halo
            sent_ref[1 - slot, side] = even_ref[pl.ds(at, halo)]

        for side in range(2):
            @pl.when(jnp.logical_and(sides[side][0], block < blocks - 1))
            def _(side=side):
                h_copy(side, 1 - slot).start()

    for source in range(quad):
        cells = even_ref[pl.ds(pad + source * rows, rows)].reshape(rows * sub, width)
        picked = None
        one_hot = one_hot_ref[source]
        for part in range(3):
            cut = cells.astype(jnp.bfloat16)
            if part < 2:
                cells = cells - cut.astype(jnp.float32)
            term = jnp.dot(cut, one_hot, preferred_element_type=jnp.float32)
            picked = term if picked is None else picked + term
        row_at, _ = place_of(source)
        at_row = lax.broadcasted_iota(jnp.int32, (rows, sub, count_obs), 0) == row_at
        pick_ref[source] = jnp.sum(
            jnp.where(at_row, picked.reshape(rows, sub, count_obs), 0.0), axis=0
        )

    def pred_copy(k, source_ens, source_pos):
        mate, other = peers[k]
        return pltpu.make_async_remote_copy(
            pick_ref.at[mate], pred_ref.at[source_ens, source_pos],
            pred_send.at[k], pred_recv.at[source_ens, source_pos],
            device_id={"space": home + mate, "ens": other}, device_id_type=MESH,
        )

    for k in range(len(peers)):
        pred_copy(k, ens, pos).start()
    pred_ref[ens, pos] = pick_ref[pos]

    def thick_copy(mate, source, slot):
        return pltpu.make_async_remote_copy(
            stage_ref.at[mate], out_ref.at[pl.ds(source * sub, sub)],
            thick_send.at[slot], thick_recv.at[source],
            device_id={"space": home + mate}, device_id_type=MESH,
        )

    def unturn(mate):
        @pl.loop(0, rows // sub)
        def _(tile):
            at = pl.multiple_of(tile * sub, sub)
            cells = even_ref[pl.ds(pad + mate * rows + at, sub)].reshape(sub * sub, width)
            stage_ref[mate, :, pl.ds(at, sub)] = jnp.swapaxes(
                to_natural(cells).reshape(sub, sub, width), 0, 1
            )

    for slot, mate in enumerate(mates):
        unturn(mate)
        thick_copy(mate, pos, slot).start()
    unturn(pos)
    own_thick = pltpu.make_async_copy(
        stage_ref.at[pos], out_ref.at[pl.ds(pos * sub, sub)], local_sem.at[9]
    )
    own_thick.start()
    for k, (mate, other) in enumerate(peers):
        pred_copy(k, other, mate).wait_recv()

    scaling = lax.rsqrt(noise_ref[...])
    predicted = pred_ref[...].reshape(every, count_obs)
    average = jnp.sum(predicted, axis=0, keepdims=True) * (1.0 / every)
    root = jnp.sqrt(jnp.float32(every - 1))
    anomalies = (predicted - average) * (scaling / root)
    surprise = (observed_ref[...] - average) * scaling
    half = every // 2
    stacked = jnp.concatenate([anomalies, jnp.broadcast_to(surprise, (sub, count_obs))], axis=0)
    gram = dot(stacked, anomalies, 1)
    vector = gram[every:]
    sum_ref[0, pl.ds(0, half)] = jnp.concatenate([gram[:half], gram[half:every]], axis=1)
    sum_ref[0, pl.ds(half, sub)] = jnp.concatenate([vector, vector], axis=1)

    def sum_copies(stage):
        return [
            pltpu.make_async_remote_copy(
                sum_ref.at[stage], sum_land.at[stage, k],
                sum_send.at[stage, k], sum_recv.at[stage, k],
                device_id={"space": partner}, device_id_type=MESH,
            )
            for k, partner in enumerate(partners[stage])
        ]

    for stage in range(len(bits)):
        for copy in sum_copies(stage):
            copy.start()
        if stage == min(1, len(bits) - 1):
            fetches[-2].wait()
            own_params.wait()
            for step in range(enss - 1):
                ens_copy(step, others[step]).wait_recv()

            @pl.loop(0, groups)
            def _(group):
                member = pl.multiple_of(lax.rem(group, quad) * sub, sub)
                turned_ref[group] = jnp.swapaxes(
                    par_ref[lax.div(group, quad), pl.ds(member, sub)], 0, 1
                )

            @pl.loop(0, rows)
            def _(row):
                values = turned_ref[:, row].reshape(every, width)
                middle = jnp.sum(turned_ref[:, row], axis=0)
                middle = jnp.sum(middle, axis=0, keepdims=True) * (1.0 / every)
                deviation = values - middle
                high = deviation.astype(jnp.bfloat16)
                parts_ref[row, pl.ds(0, every)] = high
                parts_ref[row, pl.ds(every, every)] = (
                    deviation - high.astype(jnp.float32)
                ).astype(jnp.bfloat16)

        added = sum_ref[stage]
        for k, copy in enumerate(sum_copies(stage)):
            copy.wait_recv()
            added = added + sum_land[stage, k]
        sum_ref[stage + 1] = added

    spread = 2 * every
    folded = sum_ref[len(bits), pl.ds(0, half)]
    row_of = lax.broadcasted_iota(jnp.int32, (every, every), 0)
    lane_of = lax.broadcasted_iota(jnp.int32, (every, every), 1)
    diagonal = row_of == lane_of
    vector = jnp.broadcast_to(sum_ref[len(bits), pl.ds(half, 1)][:, :every], (every, every))
    vector = jnp.sum(jnp.where(diagonal, vector, 0.0), axis=1, keepdims=True)
    own_unit = (row_of == lane_of + (ens * members - 1)) & (lane_of > 0)
    system = jnp.concatenate([
        jnp.concatenate([folded[:, :every], folded[:, every:]], axis=0)
        + jnp.where(diagonal, 1.0, 0.0),
        jnp.where(lane_of == 0, vector, jnp.where(own_unit, 1.0, 0.0)),
    ], axis=1)
    row_of = lax.broadcasted_iota(jnp.int32, (every, spread), 0)
    for pivot in range(0, every, 4):
        four = range(4)
        columns = [
            jnp.broadcast_to(system[:, pivot + k : pivot + k + 1], (every, spread)) for k in four
        ]
        lines = [system[pivot + k : pivot + k + 1] for k in four]
        m = [[columns[j][pivot + i : pivot + i + 1] for j in four] for i in four]
        scale = 1.0 / (m[0][0] * m[1][1] - m[0][1] * m[1][0])

        def first_pair(x, y, m=m, scale=scale):
            return (m[1][1] * x - m[0][1] * y) * scale, (m[0][0] * y - m[1][0] * x) * scale

        b = [first_pair(m[0][k], m[1][k]) for k in (2, 3)]
        new = list(first_pair(lines[0], lines[1]))
        d = [[m[i][2 + k] - m[i][0] * b[k][0] - m[i][1] * b[k][1] for k in (0, 1)] for i in (2, 3)]
        y = [lines[i] - m[i][0] * new[0] - m[i][1] * new[1] for i in (2, 3)]
        scale = 1.0 / (d[0][0] * d[1][1] - d[0][1] * d[1][0])
        new.append((d[1][1] * y[0] - d[0][1] * y[1]) * scale)
        new.append((d[0][0] * y[1] - d[1][0] * y[0]) * scale)
        for i in (0, 1):
            new[i] = new[i] - b[0][i] * new[2] - b[1][i] * new[3]
        rest = system
        for k in four:
            rest = rest - columns[k] * new[k]
        for k in four:
            rest = jnp.where(row_of == pivot + k, new[k], rest)
        system = rest
    gain = system[:, every : every + 1] / root
    weights = system[:, every + 1 : every + 1 + members] + gain
    weights = weights - jnp.where(
        lax.broadcasted_iota(jnp.int32, (every, members), 0)
        == lax.broadcasted_iota(jnp.int32, (every, members), 1) + ens * members, 1.0, 0.0,
    )
    weights = weights.T
    high = weights.astype(jnp.bfloat16)
    low = (weights - high.astype(jnp.float32)).astype(jnp.bfloat16)
    weights_ref[...] = jnp.concatenate([
        jnp.concatenate([high, high], axis=1), jnp.concatenate([low, low], axis=1)
    ], axis=0)

    for mate in mates:
        thick_copy(mate, mate, 0).wait_recv()
    own_thick.wait()
    for slot, mate in enumerate(mates):
        for which in range(2):
            if slot == 1:
                bb_copy(which, twin, far[0], slot, True).wait_send()
            else:
                bb_copy(which, mate, pos, slot).wait_send()
        raw_copy(mate, pos, slot).wait_send()
        index_copy(mate, pos, slot).wait_send()
        thick_copy(mate, pos, slot).wait_send()
    for step in range(enss - 1):
        ens_copy(step, ens).wait_send()
    for k in range(len(peers)):
        pred_copy(k, ens, pos).wait_send()
    for stage in range(len(bits)):
        for copy in sum_copies(stage):
            copy.wait_send()
    for side in range(2):
        @pl.when(sides[side][0])
        def _(side=side):
            for copy in edge_copies(side):
                copy.wait_send()
            h_copy(side, (blocks - 1) % 2).wait_send()


def finish_kernel(thick_ref, params_ref, parts_ref, weights_ref, out_ref, updated_ref, made_ref, sem):
    members, rows, width = params_ref.shape
    quad = members // sub
    thick = pltpu.make_async_copy(thick_ref, out_ref, sem.at[0])
    thick.start()
    weights = weights_ref[...]
    copies = []
    for tile in range(rows // sub):
        here = pl.ds(tile * sub, sub)
        steps_made = []
        for k in range(sub):
            both = jnp.dot(
                weights, parts_ref[tile * sub + k], preferred_element_type=jnp.float32
            )
            steps_made.append(both[:members] + both[members:])
        for group in range(quad):
            own = slice(group * sub, (group + 1) * sub)
            made = jnp.stack([step[own] for step in steps_made])
            there = pl.ds(group * sub, sub)
            made_ref[there, here] = params_ref[there, here] + jnp.swapaxes(made, 0, 1)
            copies.append(pltpu.make_async_copy(
                made_ref.at[there, here], updated_ref.at[there, here], sem.at[1 + len(copies)]
            ))
            copies[-1].start()
    for copy in copies:
        copy.wait()
    thick.wait()


def shards(params, base_thickness, balance, step_count, obs_index, observed, noise_var):
    members, rows, width = params.shape
    spaces, enss = lax.axis_size("space"), lax.axis_size("ens")
    quad = members // sub
    total = quad * rows
    every = members * enss
    count_obs = obs_index.shape[0]
    stages = spaces.bit_length() - 1
    assert 1 << stages == spaces and spaces % quad == 0 and quad in (1, 2, 4)
    assert 2 * every == lane and members < every
    assert width & (width - 1) == 0 and steps // halo > 2
    dma = pltpu.SemaphoreType.DMA
    vmem = pl.BlockSpec(memory_space=pltpu.VMEM)
    f32 = jnp.float32
    many = max(quad - 1, 1)
    flat = jax.ShapeDtypeStruct(params.shape, f32)
    thick, parts, weights, own = pl.pallas_call(
        functools.partial(kernel, spaces, enss),
        out_shape=(
            flat,
            jax.ShapeDtypeStruct((rows, 2 * every, width), jnp.bfloat16),
            jax.ShapeDtypeStruct((2 * members, 2 * every), jnp.bfloat16),
            flat,
        ),
        in_specs=[pl.BlockSpec(memory_space=pltpu.HBM)] * 7,
        out_specs=(vmem,) * 4,
        scratch_shapes=[
            pltpu.VMEM((1, every), jnp.int32),
            pltpu.VMEM((1, count_obs), f32),
            pltpu.VMEM((1, count_obs), f32),
            pltpu.VMEM((quad, sub, rows, width), f32),
            pltpu.VMEM((enss, members, rows, width), f32),
            pltpu.VMEM((2, quad, rows, width), f32),
            pltpu.VMEM((quad, 1, count_obs), jnp.int32),
            pltpu.VMEM((total + 2 * pad, sub, width), f32),
            pltpu.VMEM((total + 2 * pad, sub, width), f32),
            pltpu.VMEM((total + 2 * pad, sub, width), f32),
            pltpu.VMEM((total + 2 * pad, width), f32),
            pltpu.VMEM((total + 2 * pad, width), f32),
            pltpu.VMEM((2, 2, halo, sub, width), f32),
            pltpu.VMEM((2, 2, halo, sub, width), f32),
            pltpu.VMEM((quad, width, count_obs), jnp.bfloat16),
            pltpu.VMEM((quad, sub, count_obs), f32),
            pltpu.VMEM((enss, quad, sub, count_obs), f32),
            pltpu.VMEM((quad, sub, rows, width), f32),
            pltpu.VMEM((quad * enss, rows, sub, width), f32),
            pltpu.VMEM((stages + 1, every // 2 + sub, 2 * every), f32),
            pltpu.VMEM((stages, 3, every // 2 + sub, 2 * every), f32),
            dma((many,)), dma((quad,)),
            dma((2, many)), dma((2, quad)),
            dma((many,)), dma((quad,)),
            dma((max(enss - 1, 1),)), dma((enss,)),
            dma((10,)),
            dma((2, 3)), dma((2, 3)),
            dma((2, 2)), dma((2, 2)),
            dma((quad * enss,)), dma((enss, quad)),
            dma((many,)), dma((quad,)),
            dma((stages, 3)), dma((stages, 3)),
        ],
        compiler_params=pltpu.CompilerParams(
            collective_id=0, has_side_effects=True, vmem_limit_bytes=48 * 1024 * 1024
        ),
        name="advance",
    )(
        *(pltpu.with_memory_space_constraint(x, pltpu.HBM) for x in (
            params, base_thickness, balance, step_count[None],
            obs_index[None], observed[None], noise_var[None],
        ))
    )
    return pl.pallas_call(
        finish_kernel,
        out_shape=(flat, flat),
        in_specs=[vmem] * 4,
        out_specs=(pl.BlockSpec(memory_space=pltpu.HBM),) * 2,
        scratch_shapes=[pltpu.VMEM(params.shape, f32), dma((1 + quad * (rows // sub),))],
        compiler_params=pltpu.CompilerParams(vmem_limit_bytes=8 * 1024 * 1024),
        name="finish",
    )(thick, own, parts, weights)


def solution(mesh):
    in_specs = (
        P("ens", "space", None),
        P("space", None),
        P("space", None),
        P(),
        P("space"),
        P("space"),
        P("space"),
    )
    out_specs = (P("ens", "space", None), P("ens", "space", None))
    return jax.shard_map(shards, mesh=mesh, in_specs=in_specs, out_specs=out_specs, check_vma=False)
```
